512 devices in a mesh: chan: 32 (over y, x, core), tile: 16 (over z).
Axes of the slice: x: 4, y: 4, z: 16, core: 2. Of those that a mesh axis runs over, the one named last changes fastest.
Arguments:
- visibility: float32 [2, 524288], P(None, ('chan', 'tile')), may hold values from -6 to 6
- kernel_table: bfloat16 [2048, 128], replicated, may hold values from -0.8984375 to 0.8984375
- cell_index: int32 [524288], P(('chan', 'tile')), may hold values from 0 to 65535
- tile_index: int32 [524288, 1], P(('chan', 'tile')), may hold values from 0 to 15; in each aligned block of 1024 rows (0 to 1023, 1024 to 2047, ...) at most 128 rows name the same one
- plane_index: int32 [524288], P(('chan', 'tile')), may hold values from 0 to 31
- offset_index: int32 [524288], P(('chan', 'tile')), may hold values from 0 to 63
Outputs:
- gridded: float32 [2, 256, 4096], P(None, 'tile', 'chan')
The draws below stay inside these ranges and needn't reach their ends.
Inputs may be any that keep to these rules, and one draw needn't show every extreme that they name: `tile_index`: among the rows of one device at most 128 name the same tile, and in some device some tile is named by exactly 128 rows.
All inputs are finite; a program needn't handle non-finite values.
Results may differ from the reference program's by a relative error of at most 0.0029.
Values may be sent and summed in bfloat16 or wider, within the bound.
A program may use at most 64 MiB of HBM per device.

```python
import math
import jax
import jax.numpy as jnp
import numpy as np
from jax import lax

GRID_U = 4096
SUPPORT = 8
OVERSAMPLE = 8
PLANES = 32
TILE_V = 16
CAPACITY = 128
ROWS_DEV = 1024
ROWS = 524288
BAND_V = 256
KERNELS = 2048
N_TILE = 16


def with_ends(values, key, least, top_value):
    shape = values.shape
    place = [jax.random.randint(jax.random.fold_in(key, axis), (), 0, shape[axis]) for axis in range(len(shape))]
    values = values.at[tuple(place)].set(least)
    longest = shape.index(max(shape))
    place[longest] = (place[longest] + 1) % shape[longest]
    return values.at[tuple(place)].set(top_value)


def steps_of(rng, extent, split, least, largest):
    factor_of, own = 1.0, jax.random.fold_in(rng, 6)
    for axis_at, blocks in split:
        draws = jnp.exp(jax.random.uniform(jax.random.fold_in(own, axis_at), (blocks,), jnp.float32, least / len(split), largest / len(split)))
        factor_of = factor_of * jnp.repeat(draws, extent[axis_at] // blocks).reshape([-1 if axis == axis_at else 1 for axis in range(len(extent))])
    return factor_of


def shared_out(own_key, own, number, rows, number_of, top, bound, skew):
    ranking = jax.random.permutation(own_key, number_of)
    packed, usual = load_shares(number_of, rows * top, bound, skew, True), load_shares(number_of, rows * top, bound, skew, False)
    places = jnp.arange(number_of)

    def named(sizes, rotation):
        used = int((sizes > 0).sum())
        fixed = max(1, used // 4)
        passed = fixed + (places - fixed + rotation * (used - fixed)) % max(1, number_of - fixed)
        return jnp.zeros((number_of,), jnp.int32).at[ranking[jnp.where(places < fixed, places, passed)]].set(jnp.asarray(sizes, jnp.int32))

    sizes = jnp.where(number % 4 == 0, named(packed, number // 4), named(usual, number - number // 4 - 1))
    mixed = jax.random.permutation(jax.random.fold_in(own, 3), number_of)
    giver, receiver = mixed[0:number_of // 2 * 2:2], mixed[1:number_of // 2 * 2:2]
    margin = jnp.minimum(sizes[giver] - 1, bound - sizes[receiver]) // 2
    margin = jnp.where((giver == ranking[0]) | (receiver == ranking[0]) | (sizes[receiver] == 0), 0, jnp.maximum(margin, 0))
    passed = jax.random.randint(jax.random.fold_in(own, 4), (number_of // 2,), 0, 1 << 20) % (margin + 1)
    sizes = sizes.at[giver].add(-passed).at[receiver].add(passed)
    items = jnp.searchsorted(jnp.cumsum(sizes), jnp.arange(rows * top), side="right").astype(jnp.int32)
    table = items.reshape(top, rows).T
    table = table[jax.random.permutation(jax.random.fold_in(own, 1), rows)]
    rotation = jax.random.randint(jax.random.fold_in(own, 2), (rows, 1), 0, top)
    return jnp.take_along_axis(table, (jnp.arange(top)[None, :] + rotation) % top, axis=1)


def load_shares(amount, total, limit, skew, full):
    portions = [(1 << 20) // math.isqrt(grade ** skew) + 1 for grade in range(1, amount + 1)]
    largest = limit if full else min(limit, max(-(-total // amount), total * portions[0] // sum(portions)))
    least = 1 if total - largest >= amount - 1 else 0
    holding, spare = [largest] + [least] * (amount - 1), total - largest - least * (amount - 1)
    while spare > 0:
        candidates = [i for i in range(1, amount) if holding[i] < largest] or [i for i in range(1, amount) if holding[i] < limit]
        whole, remaining = sum([portions[i] for i in candidates]), spare
        for i in candidates:
            extra = min(limit - holding[i], max(1, remaining * portions[i] // whole), spare)
            holding[i] = holding[i] + extra
            spare = spare - extra
    return np.array(holding)


def centred(key, shape, scale, reach, shards=(), kind=jnp.bfloat16):
    gain = steps_of(key, shape, shards, -0.22, 0.18) if shards else 1.0
    result = jax.random.normal(key, shape, jnp.float32) * scale * gain
    return jnp.minimum(jnp.maximum(result, -reach), reach).astype(kind)


def setup_inputs(seed: int = 0) -> dict:
    seeds = jax.random.split(jax.random.key(seed), 7)
    visibility = centred(seeds[0], (2, ROWS), 1.0, 6.0, ((1, 512),), jnp.float32)
    kernel_table = centred(seeds[1], (KERNELS, 2 * SUPPORT * SUPPORT), 0.15, 0.8984375)
    cell_index = with_ends(jax.random.randint(seeds[2], (ROWS,), 0, TILE_V * GRID_U), jax.random.fold_in(seeds[2], 1), 0, (TILE_V * GRID_U) - 1).astype(jnp.int32)
    tile_index_keys = jax.random.split(jax.random.fold_in(seeds[3], 1), ROWS // ROWS_DEV)
    tile_index_turns = jax.random.permutation(jax.random.fold_in(seeds[3], 3), ROWS // ROWS_DEV)
    tile_index = jax.vmap(lambda own, number: shared_out(jax.random.fold_in(seeds[3], 2), own, number, ROWS_DEV, N_TILE, 1, CAPACITY, 2))(tile_index_keys, tile_index_turns).reshape((ROWS, 1))
    plane_index = with_ends(jax.random.randint(seeds[4], (ROWS,), 0, PLANES), jax.random.fold_in(seeds[4], 1), 0, PLANES - 1).astype(jnp.int32)
    offset_index = with_ends(jax.random.randint(seeds[5], (ROWS,), 0, OVERSAMPLE * OVERSAMPLE), jax.random.fold_in(seeds[5], 1), 0, (OVERSAMPLE * OVERSAMPLE) - 1).astype(jnp.int32)
    return dict(visibility=visibility, kernel_table=kernel_table, cell_index=cell_index, tile_index=tile_index, plane_index=plane_index, offset_index=offset_index)


def reference(visibility, kernel_table, cell_index, tile_index, plane_index, offset_index):
    kind = plane_index * (OVERSAMPLE * OVERSAMPLE) + offset_index
    area = SUPPORT * SUPPORT
    blocks = ROWS // ROWS_DEV
    vis_blocks = visibility.reshape(2, blocks, ROWS_DEV).transpose(1, 0, 2)
    kind_blocks = kind.reshape(blocks, ROWS_DEV)
    cell_blocks = cell_index.reshape(blocks, ROWS_DEV)
    tile_blocks = tile_index[:, 0].reshape(blocks, ROWS_DEV)
    taps = jnp.arange(SUPPORT, dtype=jnp.int32)

    def step(grid, pieces):
        vis_part, kind_part, cell_part, tile_part = pieces
        kern = kernel_table[kind_part].astype(jnp.float32)
        real_kern = kern[:, :area]
        imag_kern = kern[:, area:]
        vis_real = vis_part[0][:, None]
        vis_imag = vis_part[1][:, None]
        real_part = (vis_real * real_kern - vis_imag * imag_kern).astype(jnp.bfloat16)
        imag_part = (vis_real * imag_kern + vis_imag * real_kern).astype(jnp.bfloat16)
        real_part, imag_part = lax.optimization_barrier((real_part, imag_part))
        real_part = real_part.astype(jnp.float32).reshape(-1, SUPPORT, SUPPORT)
        imag_part = imag_part.astype(jnp.float32).reshape(-1, SUPPORT, SUPPORT)
        row_pos = tile_part * TILE_V + cell_part // GRID_U
        col_pos = cell_part % GRID_U
        ys = jnp.broadcast_to(row_pos[:, None, None] + taps[None, None, :], real_part.shape).astype(jnp.int32)
        xs = jnp.broadcast_to(col_pos[:, None, None] + taps[None, :, None], real_part.shape).astype(jnp.int32)
        grid = grid.at[0, ys, xs].add(real_part, mode="drop")
        grid = grid.at[1, ys, xs].add(imag_part, mode="drop")
        return grid, None

    start = jnp.zeros((2, BAND_V, GRID_U), jnp.float32)
    grid, _ = lax.scan(step, start, (vis_blocks, kind_blocks, cell_blocks, tile_blocks))
    return grid
```

```python
import functools

import jax
import jax.numpy as jnp
from jax import lax
from jax.experimental import pallas as pl
from jax.experimental.pallas import tpu as pltpu
from jax.sharding import PartitionSpec as P

SUPPORT = 8
TILE_V = 16
CAPACITY = 128
SUB_V = 24
LANES = 128
AREA = SUPPORT * SUPPORT
FIELDS = 16
LOW = 512
GROUP = 4

NT = (((1,), (1,)), ((), ()))


def iota(shape, axis):
    return lax.broadcasted_iota(jnp.int32, shape, axis)


def zigzag(size):
    order = [0]
    for step in range(1, size // 2 + 1):
        order.append(step)
        if size - step != step:
            order.append(size - step)
    return order


def kernel(chans, tiles, vis_ref, cell_ref, tile_ref, plane_ref, offset_ref, table_ref, out_ref,
           rows, ranks, table, lookup, send_rows, got_rows, spread, onehot, sums, send_part, got_part,
           edge, got_edge, table_sem, row_send, row_recv, part_send, part_recv, edge_send, edge_recv):
    chan = lax.axis_index("chan")
    tile = lax.axis_index("tile")
    width = chans * LANES
    coarse = width // SUPPORT
    blocks = tile_ref.shape[0]

    barrier = pltpu.get_barrier_semaphore()
    for k in range(1, tiles):
        pl.semaphore_signal(barrier, inc=1, device_id={"tile": lax.rem(tile + k, tiles)},
                            device_id_type=pl.DeviceIdType.MESH)
    for k in range(1, chans):
        pl.semaphore_signal(barrier, inc=1, device_id={"chan": lax.rem(chan + k, chans)},
                            device_id_type=pl.DeviceIdType.MESH)
    fetch = pltpu.make_async_copy(table_ref, table, table_sem)
    fetch.start()

    owner = tile_ref[...]
    marks = jnp.concatenate([jnp.where(owner == t, 1.0, 0.0) for t in range(tiles)], axis=0)
    size = tiles * blocks
    marks16 = marks.astype(jnp.bfloat16)
    before = jnp.where(iota((LANES, LANES), 0) < iota((LANES, LANES), 1), 1.0, 0.0).astype(jnp.bfloat16)
    inside = jnp.dot(marks16, before, preferred_element_type=jnp.float32)
    totals = jnp.dot(marks16, jnp.ones((LANES, LANES), jnp.bfloat16), preferred_element_type=jnp.float32)
    here, there = iota((size, size), 0), iota((size, size), 1)
    earlier = jnp.where((here // blocks == there // blocks) & (there < here), 1.0, 0.0).astype(jnp.bfloat16)
    ahead = jnp.dot(earlier, totals.astype(jnp.bfloat16), preferred_element_type=jnp.float32)
    ranks[...] = jnp.where(marks > 0.5, inside + ahead, -1.0)

    cell = cell_ref[...]
    u = cell & (width - 1)
    v = cell // width
    fields = [plane_ref[...], offset_ref[...], v, u // LANES, u & (LANES - 1)]
    rows[...] = jnp.zeros_like(rows)
    vis = vis_ref[...]
    high = vis.astype(jnp.bfloat16).astype(jnp.float32)
    low = vis - high
    rows[0:2, :] = high
    rows[2:4, :] = low
    for at, field in enumerate(fields):
        field = field.astype(jnp.float32)
        for b in range(blocks):
            rows[4 + at : 5 + at, b * LANES : (b + 1) * LANES] = field[b : b + 1, :]
    rows16 = rows[...].astype(jnp.bfloat16)

    slot = iota((CAPACITY, LANES), 0).astype(jnp.float32)
    for t in range(tiles):
        pick = jnp.concatenate(
            [
                jnp.where(slot == ranks[t * blocks + b : t * blocks + b + 1, :], 1.0, 0.0).astype(jnp.bfloat16)
                for b in range(blocks)
            ],
            axis=1,
        )
        send_rows[t] = lax.dot_general(rows16, pick, NT, preferred_element_type=jnp.float32).astype(jnp.bfloat16)

    pl.semaphore_wait(barrier, tiles - 1 + chans - 1)
    row_copies = []
    order = zigzag(tiles)
    for j in range(1, tiles):
        to = lax.rem(tile + order[j], tiles)
        copy = pltpu.make_async_remote_copy(
            src_ref=send_rows.at[to], dst_ref=got_rows.at[j], send_sem=row_send.at[j], recv_sem=row_recv.at[j],
            device_id={"tile": to}, device_id_type=pl.DeviceIdType.MESH)
        copy.start()
        row_copies.append(copy)
    got_rows[0] = send_rows[tile]

    fetch.wait()
    high_kinds = table.shape[0] // LOW
    for h in range(high_kinds):
        lookup[h * LANES : (h + 1) * LANES, :] = table[h * LOW : (h + 1) * LOW, :].T

    sums[0:8, :] = jnp.zeros((8, sums.shape[1]), jnp.float32)
    chunk = GROUP * CAPACITY
    for q in range(tiles // GROUP):
        for j in range(q * GROUP, (q + 1) * GROUP):
            if j > 0:
                row_copies[j - 1].wait_recv()
        lanes = slice(q * chunk, (q + 1) * chunk)
        got = jnp.concatenate([got_rows[q * GROUP + j].astype(jnp.float32) for j in range(GROUP)], axis=1)
        real, imag = got[0:1] + got[2:3], got[1:2] + got[3:4]
        whole = got.astype(jnp.int32)
        plane, offset, v, u_high, u_low = (whole[4 + k : 5 + k] for k in range(5))
        kind_high = plane // 8
        kind_low = (plane & 7) * 64 + offset
        pick = jnp.where(iota((LOW, chunk), 0) == kind_low, 1.0, 0.0).astype(jnp.bfloat16)
        found = jnp.dot(lookup[...], pick, preferred_element_type=jnp.float32)
        kern = found[0:LANES]
        for h in range(1, high_kinds):
            kern = jnp.where(kind_high == h, found[h * LANES : (h + 1) * LANES], kern)
        kern_real, kern_imag = kern[:AREA], kern[AREA:]
        parts = [real * kern_real - imag * kern_imag, real * kern_imag + imag * kern_real]
        parts = [part.astype(jnp.bfloat16).astype(jnp.float32) for part in parts]

        onehot[:, lanes] = jnp.where(
            iota((coarse, chunk), 0) == u_high * (LANES // SUPPORT) + u_low // SUPPORT, 1.0, 0.0
        ).astype(jnp.bfloat16)
        fine = u_low & (SUPPORT - 1)
        row = iota((8, chunk), 0)
        zero = jnp.zeros((8, chunk), jnp.float32)
        turned = []
        for part in parts:
            taps = [part[8 * i : 8 * i + 8] for i in range(SUPPORT)]
            for bit in range(3):
                on = (v & (1 << bit)) != 0
                taps = [jnp.where(on, pltpu.roll(tap, 1 << bit, 0), tap) for tap in taps]
            for bit in range(3):
                by = 1 << bit
                on = (fine & by) != 0
                shifted = [zero] * by + taps
                kept = taps + [zero] * by
                taps = [jnp.where(on, a, b) for a, b in zip(shifted, kept)]
            turned.append(taps)
        keep = [(row + 8 * k >= v) & (row + 8 * k < v + SUPPORT) for k in range(SUB_V // 8)]
        for f in range(2 * SUPPORT):
            if f < 2 * SUPPORT - 1:
                stack = [jnp.where(keep[k], turned[c][f], 0.0) for c in range(2) for k in range(SUB_V // 8)]
            else:
                stack = [zero] * (2 * SUB_V // 8)
            spread[f * 2 * SUB_V : (f + 1) * 2 * SUB_V, lanes] = jnp.concatenate(stack, axis=0).astype(jnp.bfloat16)

    half = SUPPORT * 2 * SUB_V
    for q in range(coarse // 128):
        sums[8 + q * 128 : 8 + (q + 1) * 128, :] = lax.dot_general(
            onehot[q * 128 : (q + 1) * 128, :], spread[...], NT, preferred_element_type=jnp.float32)
        piece = sums[8 + q * 128 : 8 + (q + 1) * 128, :half] + sums[7 + q * 128 : 7 + (q + 1) * 128, half:]
        for k in range(8):
            send_part[q * 8 + k] = piece[k * 16 : (k + 1) * 16].astype(jnp.bfloat16)

    part_copies = []
    for k in range(1, chans):
        to = lax.rem(chan + k, chans)
        copy = pltpu.make_async_remote_copy(
            src_ref=send_part.at[to], dst_ref=got_part.at[k], send_sem=part_send.at[k], recv_sem=part_recv.at[k],
            device_id={"chan": to}, device_id_type=pl.DeviceIdType.MESH)
        copy.start()
        part_copies.append(copy)
    total = send_part[chan].astype(jnp.float32)
    for k in range(1, chans):
        part_copies[k - 1].wait_recv()
        total = total + got_part[k].astype(jnp.float32)

    turned = total.T
    cols = LANES // SUPPORT
    grid = jnp.zeros((2 * SUB_V, LANES), jnp.float32)
    for f in range(SUPPORT):
        place = jnp.where(iota((cols, LANES), 1) == SUPPORT * iota((cols, LANES), 0) + f, 1.0, 0.0)
        grid = grid + jnp.dot(turned[f * 2 * SUB_V : (f + 1) * 2 * SUB_V], place,
                              precision=lax.Precision.HIGHEST, preferred_element_type=jnp.float32)
    for c in range(2):
        edge[c] = grid[c * SUB_V + TILE_V : (c + 1) * SUB_V]
    copy = pltpu.make_async_remote_copy(
        src_ref=edge, dst_ref=got_edge, send_sem=edge_send, recv_sem=edge_recv,
        device_id={"tile": lax.rem(tile + 1, tiles)}, device_id_type=pl.DeviceIdType.MESH)
    copy.start()
    for c in range(2):
        out_ref[c, SUPPORT:, :] = grid[c * SUB_V + SUPPORT : c * SUB_V + TILE_V]
    for other in row_copies + part_copies:
        other.wait_send()
    copy.wait()
    used = jnp.where(tile > 0, 1.0, 0.0)
    for c in range(2):
        out_ref[c, :SUPPORT, :] = grid[c * SUB_V : c * SUB_V + SUPPORT] + used * got_edge[c]


def body(visibility, kernel_table, cell_index, tile_index, plane_index, offset_index):
    chans, tiles = lax.axis_size("chan"), lax.axis_size("tile")
    count = cell_index.shape[0]
    blocks = count // LANES
    shape = (blocks, LANES)
    slots = tiles * CAPACITY
    coarse = chans * LANES // SUPPORT
    lanes = 2 * SUPPORT * 2 * SUB_V
    cols = LANES // SUPPORT
    vmem = pl.BlockSpec(memory_space=pltpu.VMEM)
    return pl.pallas_call(
        functools.partial(kernel, chans, tiles),
        out_shape=jax.ShapeDtypeStruct((2, TILE_V, LANES), jnp.float32),
        in_specs=[vmem] * 5 + [pl.BlockSpec(memory_space=pl.ANY)],
        out_specs=vmem,
        scratch_shapes=[
            pltpu.VMEM((FIELDS, count), jnp.float32),
            pltpu.VMEM((tiles * blocks, LANES), jnp.float32),
            pltpu.VMEM(kernel_table.shape, kernel_table.dtype),
            pltpu.VMEM((kernel_table.shape[0] // LOW * LANES, LOW), jnp.bfloat16),
            pltpu.VMEM((tiles, FIELDS, CAPACITY), jnp.bfloat16),
            pltpu.VMEM((tiles, FIELDS, CAPACITY), jnp.bfloat16),
            pltpu.VMEM((lanes, slots), jnp.bfloat16),
            pltpu.VMEM((coarse, slots), jnp.bfloat16),
            pltpu.VMEM((8 + coarse, lanes), jnp.float32),
            pltpu.VMEM((chans, cols, lanes // 2), jnp.bfloat16),
            pltpu.VMEM((chans, cols, lanes // 2), jnp.bfloat16),
            pltpu.VMEM((2, SUPPORT, LANES), jnp.float32),
            pltpu.VMEM((2, SUPPORT, LANES), jnp.float32),
            pltpu.SemaphoreType.DMA,
            pltpu.SemaphoreType.DMA((tiles,)),
            pltpu.SemaphoreType.DMA((tiles,)),
            pltpu.SemaphoreType.DMA((chans,)),
            pltpu.SemaphoreType.DMA((chans,)),
            pltpu.SemaphoreType.DMA,
            pltpu.SemaphoreType.DMA,
        ],
        compiler_params=pltpu.CompilerParams(
            collective_id=0, has_side_effects=True, vmem_limit_bytes=48 * 1024 * 1024),
    )(visibility, cell_index.reshape(shape), tile_index.reshape(shape), plane_index.reshape(shape),
      offset_index.reshape(shape), kernel_table)


def solution(mesh):
    placed = (
        P(None, ("chan", "tile")),
        P(),
        P(("chan", "tile")),
        P(("chan", "tile"), None),
        P(("chan", "tile")),
        P(("chan", "tile")),
    )
    return jax.shard_map(
        body, mesh=mesh, in_specs=placed, out_specs=P(None, "tile", "chan"), check_vma=False
    )
```

```python
import functools

import jax
import jax.numpy as jnp
from jax import lax
from jax.experimental import pallas as pl
from jax.experimental.pallas import tpu as pltpu
from jax.sharding import PartitionSpec as P

SUPPORT = 8
TILE_V = 16
CAPACITY = 128
LANES = 128
AREA = SUPPORT * SUPPORT
FIELDS = 8
LOW = 512
GROUP = 4
COLS = LANES // SUPPORT
MAIN = SUPPORT * 2 * TILE_V
EDGE = SUPPORT * 2 * SUPPORT
HALF = MAIN + EDGE
CHIPS_X = 4
CORES = 2
NEAR = CHIPS_X * CORES
BLOCK = NEAR * COLS
MESH = pl.DeviceIdType.MESH
NT = (((1,), (1,)), ((), ()))


def iota(shape, axis):
    return lax.broadcasted_iota(jnp.int32, shape, axis)


def ones_where(mask):
    return jnp.where(mask, 1.0, 0.0).astype(jnp.bfloat16)


def near_first(size):
    return sorted(range(size), key=lambda step: min(step, size - step))


def kernel(chans, tiles, vis_hbm, cell_hbm, tile_hbm, plane_hbm, offset_hbm, table_hbm, out_ref,
           vis_ref, cell_ref, tile_ref, plane_ref, offset_ref, table, rows, ranks, lookup,
           send_rows, got_rows, spread, onehot, sums, last, send_main, got_main, send_edge, got_edge,
           load_sem, row_send, row_recv, main_send, main_recv, edge_send, edge_recv):
    chan = lax.axis_index("chan")
    tile = lax.axis_index("tile")
    chips_y = chans // NEAR
    at_y, at_x, at_core = chan // NEAR, lax.rem(chan // CORES, CHIPS_X), lax.rem(chan, CORES)
    next_tile, prev_tile = lax.rem(tile + 1, tiles), lax.rem(tile + tiles - 1, tiles)
    width = chans * LANES
    coarse = chans * COLS
    blocks = tile_ref.shape[0]

    barrier = pltpu.get_barrier_semaphore()
    for step in reversed(near_first(tiles)[1:]):
        pl.semaphore_signal(barrier, inc=1, device_id={"tile": lax.rem(tile + step, tiles)}, device_id_type=MESH)
    for k in range(1, chans):
        other = lax.rem(chan + k, chans)
        pl.semaphore_signal(barrier, inc=1, device_id={"chan": other}, device_id_type=MESH)
        for z in (next_tile, prev_tile):
            pl.semaphore_signal(barrier, inc=1, device_id={"chan": other, "tile": z}, device_id_type=MESH)
    loads = [
        pltpu.make_async_copy(source, target, load_sem.at[at])
        for at, (source, target) in enumerate(
            [(tile_hbm, tile_ref), (cell_hbm, cell_ref), (plane_hbm, plane_ref),
             (offset_hbm, offset_ref), (vis_hbm, vis_ref), (table_hbm, table)]
        )
    ]
    for load in loads:
        load.start()

    loads[0].wait()
    owner = tile_ref[...]
    marks = jnp.concatenate([jnp.where(owner == t, 1.0, 0.0) for t in range(tiles)], axis=0)
    size = tiles * blocks
    marks16 = marks.astype(jnp.bfloat16)
    before = ones_where(iota((LANES, LANES), 0) < iota((LANES, LANES), 1))
    inside = jnp.dot(marks16, before, preferred_element_type=jnp.float32)
    totals = jnp.dot(marks16, jnp.ones((LANES, LANES), jnp.bfloat16), preferred_element_type=jnp.float32)
    here, there = iota((size, size), 0), iota((size, size), 1)
    earlier = ones_where((here // blocks == there // blocks) & (there < here))
    ahead = jnp.dot(earlier, totals.astype(jnp.bfloat16), preferred_element_type=jnp.float32)
    ranks[...] = jnp.where(marks > 0.5, inside + ahead, -1.0)

    for load in loads[1:5]:
        load.wait()
    cell = cell_ref[...]
    vis = vis_ref[...]
    high = vis.astype(jnp.bfloat16).astype(jnp.float32)
    rows[0:2, :] = high
    rows[2:4, :] = vis - high
    for at, field in enumerate([plane_ref[...], offset_ref[...], cell // 256, cell & 255]):
        field = field.astype(jnp.float32)
        for b in range(blocks):
            rows[4 + at : 5 + at, b * LANES : (b + 1) * LANES] = field[b : b + 1, :]
    rows16 = rows[...].astype(jnp.bfloat16)

    slot = iota((CAPACITY, LANES), 0).astype(jnp.float32)
    for t in range(tiles):
        pick = jnp.concatenate(
            [ones_where(slot == ranks[t * blocks + b : t * blocks + b + 1, :]) for b in range(blocks)], axis=1)
        send_rows[t] = lax.dot_general(rows16, pick, NT, preferred_element_type=jnp.float32).astype(jnp.bfloat16)

    pl.semaphore_wait(barrier, tiles - 1 + 3 * (chans - 1))
    order = near_first(tiles)
    row_copies = {}
    for j in reversed(range(1, tiles)):
        to = lax.rem(tile + order[j], tiles)
        row_copies[j] = pltpu.make_async_remote_copy(
            src_ref=send_rows.at[to], dst_ref=got_rows.at[j], send_sem=row_send.at[j], recv_sem=row_recv.at[j],
            device_id={"tile": to}, device_id_type=MESH)
        row_copies[j].start()
    got_rows[0] = send_rows[tile]

    loads[5].wait()
    highs = table.shape[0] // LOW
    for h in range(highs):
        lookup[h * LANES : (h + 1) * LANES, :] = table[h * LOW : (h + 1) * LOW, :].T

    sums[0:COLS, :] = jnp.zeros((COLS, 2 * HALF), jnp.float32)
    onehot[0:COLS, :] = jnp.zeros((COLS, GROUP * CAPACITY), jnp.bfloat16)
    copies = []
    chunk = GROUP * CAPACITY
    for q in range(tiles // GROUP):
        for j in range(q * GROUP, (q + 1) * GROUP):
            if j > 0:
                row_copies[j].wait_recv()
        got = jnp.concatenate([got_rows[q * GROUP + j].astype(jnp.float32) for j in range(GROUP)], axis=1)
        real, imag = got[0:1] + got[2:3], got[1:2] + got[3:4]
        whole = got.astype(jnp.int32)
        plane, offset = whole[4:5], whole[5:6]
        cell = whole[6:7] * 256 + whole[7:8]
        u, v = cell & (width - 1), cell // width
        pick = ones_where(iota((LOW, chunk), 0) == (plane & 7) * 64 + offset)
        found = jnp.dot(lookup[...], pick, preferred_element_type=jnp.float32)
        kern = found[0:LANES]
        for h in range(1, highs):
            kern = jnp.where(plane // 8 == h, found[h * LANES : (h + 1) * LANES], kern)
        kern_real, kern_imag = kern[:AREA], kern[AREA:]
        parts = [real * kern_real - imag * kern_imag, real * kern_imag + imag * kern_real]
        parts = [part.astype(jnp.bfloat16).astype(jnp.float32) for part in parts]

        onehot[COLS:, :] = ones_where(iota((coarse, chunk), 0) == u // SUPPORT)
        fine = u & (SUPPORT - 1)
        row = iota((SUPPORT, chunk), 0)
        zero = jnp.zeros((SUPPORT, chunk), jnp.float32)
        turned = []
        for part in parts:
            taps = [part[8 * i : 8 * i + 8] for i in range(SUPPORT)]
            for bit in range(3):
                on = (v & (1 << bit)) != 0
                taps = [jnp.where(on, pltpu.roll(tap, 1 << bit, 0), tap) for tap in taps]
            for bit in range(3):
                by = 1 << bit
                on = (fine & by) != 0
                shifted = [zero] * by + taps
                kept = taps + [zero] * by
                taps = [jnp.where(on, a, b) for a, b in zip(shifted, kept)]
            turned.append(taps + [zero])
        keep = [(row + 8 * k >= v) & (row + 8 * k < v + SUPPORT) for k in range(3)]
        for f in range(2 * SUPPORT):
            base, place = f // SUPPORT * HALF, f % SUPPORT
            own = [jnp.where(keep[k], turned[c][f], 0.0) for c in range(2) for k in range(2)]
            past = [jnp.where(keep[2], turned[c][f], 0.0) for c in range(2)]
            at = base + place * 2 * TILE_V
            spread[at : at + 2 * TILE_V, :] = jnp.concatenate(own, axis=0).astype(jnp.bfloat16)
            at = base + MAIN + place * 2 * SUPPORT
            spread[at : at + 2 * SUPPORT, :] = jnp.concatenate(past, axis=0).astype(jnp.bfloat16)

        if q < tiles // GROUP - 1:
            add = lax.dot_general(onehot[COLS:, :], spread[...], NT, preferred_element_type=jnp.float32)
            sums[COLS:, :] = add if q == 0 else sums[COLS:, :] + add
            continue
        for dy in reversed(near_first(chips_y)):
            to_y = lax.rem(at_y + dy, chips_y)
            window = pl.ds(pl.multiple_of(to_y * BLOCK, BLOCK), BLOCK + COLS)
            last[...] = sums[window, :] + lax.dot_general(
                onehot[window, :], spread[...], NT, preferred_element_type=jnp.float32)
            piece = (last[COLS:, :HALF] + last[COLS - 1 : -1, HALF:]).astype(jnp.bfloat16)
            for k in range(NEAR):
                send_main[to_y * NEAR + k] = piece[k * COLS : (k + 1) * COLS, :MAIN]
                send_edge[to_y * NEAR + k] = piece[k * COLS : (k + 1) * COLS, MAIN:]
            for dx in reversed(near_first(CHIPS_X)):
                for dc in range(CORES):
                    k = dy * NEAR + dx * CORES + dc
                    to = to_y * NEAR + lax.rem(at_x + dx, CHIPS_X) * CORES + lax.rem(at_core + dc, CORES)
                    copies.append(pltpu.make_async_remote_copy(
                        src_ref=send_edge.at[to], dst_ref=got_edge.at[k], send_sem=edge_send.at[k],
                        recv_sem=edge_recv.at[k], device_id={"chan": to, "tile": next_tile}, device_id_type=MESH))
                    copies[-1].start()
                    if k > 0:
                        copies.append(pltpu.make_async_remote_copy(
                            src_ref=send_main.at[to], dst_ref=got_main.at[k], send_sem=main_send.at[k],
                            recv_sem=main_recv.at[k], device_id={"chan": to}, device_id_type=MESH))
                        copies[-1].start()

    got_main[0] = send_main[chan]
    for copy in copies:
        copy.wait_recv()
    main, past = got_main[0].astype(jnp.float32), got_edge[0].astype(jnp.float32)
    for k in range(1, chans):
        main = main + got_main[k].astype(jnp.float32)
        past = past + got_edge[k].astype(jnp.float32)
    past = jnp.where(tile > 0, past, 0.0)

    main, past = main.T, past.T
    strips = []
    for f in range(SUPPORT):
        own = main[f * 2 * TILE_V : (f + 1) * 2 * TILE_V]
        edge = past[f * 2 * SUPPORT : (f + 1) * 2 * SUPPORT]
        strips.append(jnp.concatenate(
            [own[0:8] + edge[0:8], own[8:16], own[16:24] + edge[8:16], own[24:32]], axis=0))
    mixed = jnp.concatenate(strips, axis=1)
    source, target = iota((LANES, LANES), 0), iota((LANES, LANES), 1)
    place = ones_where(target == (source & (COLS - 1)) * SUPPORT + source // COLS)
    grid = jnp.zeros((2 * TILE_V, LANES), jnp.float32)
    for _ in range(3):
        term = mixed.astype(jnp.bfloat16)
        grid = grid + jnp.dot(term, place, preferred_element_type=jnp.float32)
        mixed = mixed - term.astype(jnp.float32)
    for c in range(2):
        out_ref[c] = grid[c * TILE_V : (c + 1) * TILE_V]
    for copy in list(row_copies.values()) + copies:
        copy.wait_send()


def body(visibility, kernel_table, cell_index, tile_index, plane_index, offset_index):
    chans, tiles = lax.axis_size("chan"), lax.axis_size("tile")
    count = cell_index.shape[0]
    blocks = count // LANES
    shape = (blocks, LANES)
    coarse = chans * COLS
    chunk = GROUP * CAPACITY
    return pl.pallas_call(
        functools.partial(kernel, chans, tiles),
        out_shape=jax.ShapeDtypeStruct((2, TILE_V, LANES), jnp.float32),
        in_specs=[pl.BlockSpec(memory_space=pltpu.HBM)] * 6,
        out_specs=pl.BlockSpec(memory_space=pltpu.VMEM),
        scratch_shapes=[
            pltpu.VMEM((2, count), jnp.float32),
            pltpu.VMEM(shape, jnp.int32),
            pltpu.VMEM(shape, jnp.int32),
            pltpu.VMEM(shape, jnp.int32),
            pltpu.VMEM(shape, jnp.int32),
            pltpu.VMEM(kernel_table.shape, kernel_table.dtype),
            pltpu.VMEM((FIELDS, count), jnp.float32),
            pltpu.VMEM((tiles * blocks, LANES), jnp.float32),
            pltpu.VMEM((kernel_table.shape[0] // LOW * LANES, LOW), jnp.bfloat16),
            pltpu.VMEM((tiles, FIELDS, CAPACITY), jnp.bfloat16),
            pltpu.VMEM((tiles, FIELDS, CAPACITY), jnp.bfloat16),
            pltpu.VMEM((2 * HALF, chunk), jnp.bfloat16),
            pltpu.VMEM((COLS + coarse, chunk), jnp.bfloat16),
            pltpu.VMEM((COLS + coarse, 2 * HALF), jnp.float32),
            pltpu.VMEM((COLS + BLOCK, 2 * HALF), jnp.float32),
            pltpu.VMEM((chans, COLS, MAIN), jnp.bfloat16),
            pltpu.VMEM((chans, COLS, MAIN), jnp.bfloat16),
            pltpu.VMEM((chans, COLS, EDGE), jnp.bfloat16),
            pltpu.VMEM((chans, COLS, EDGE), jnp.bfloat16),
            pltpu.SemaphoreType.DMA((6,)),
            pltpu.SemaphoreType.DMA((tiles,)),
            pltpu.SemaphoreType.DMA((tiles,)),
            pltpu.SemaphoreType.DMA((chans,)),
            pltpu.SemaphoreType.DMA((chans,)),
            pltpu.SemaphoreType.DMA((chans,)),
            pltpu.SemaphoreType.DMA((chans,)),
        ],
        compiler_params=pltpu.CompilerParams(
            collective_id=0, has_side_effects=True, vmem_limit_bytes=60 * 1024 * 1024),
    )(visibility, cell_index.reshape(shape), tile_index.reshape(shape), plane_index.reshape(shape),
      offset_index.reshape(shape), kernel_table)


def solution(mesh):
    placed = (
        P(None, ("chan", "tile")),
        P(),
        P(("chan", "tile")),
        P(("chan", "tile"), None),
        P(("chan", "tile")),
        P(("chan", "tile")),
    )
    return jax.shard_map(
        body, mesh=mesh, in_specs=placed, out_specs=P(None, "tile", "chan"), check_vma=False
    )
```

```python
import functools

import jax
import jax.numpy as jnp
from jax import lax
from jax.experimental import pallas as pl
from jax.experimental.pallas import tpu as pltpu
from jax.sharding import PartitionSpec as P

SUPPORT = 8
TILE_V = 16
CAPACITY = 128
LANES = 128
AREA = SUPPORT * SUPPORT
FIELDS = 8
LOW = 512
WIDEST = 4
COLS = LANES // SUPPORT
MAIN = SUPPORT * 2 * TILE_V
EDGE = SUPPORT * 2 * SUPPORT
HALF = MAIN + EDGE
CHIPS_X = 4
CORES = 2
NEAR = CHIPS_X * CORES
BLOCK = NEAR * COLS
MESH = pl.DeviceIdType.MESH
NT = (((1,), (1,)), ((), ()))


def iota(shape, axis):
    return lax.broadcasted_iota(jnp.int32, shape, axis)


def ones_where(mask):
    return jnp.where(mask, 1.0, 0.0).astype(jnp.bfloat16)


def groups_of(tiles):
    bounds = [0] + list(range(1, tiles, WIDEST)) + [tiles]
    return list(zip(bounds[:-1], bounds[1:]))


def turned(tap, v, turn):
    for bit in range(3):
        tap = jnp.where((v & (1 << bit)) != 0, pltpu.roll(tap, 1 << bit, 0), tap)
    return tap


def near_first(size):
    return sorted(range(size), key=lambda step: min(step, size - step))


def kernel(chans, tiles, vis_hbm, cell_hbm, tile_hbm, plane_hbm, offset_hbm, table_hbm, out_ref,
           vis_ref, cell_ref, tile_ref, plane_ref, offset_ref, table, rows, ranks, lookup,
           send_rows, got_rows, spread, onehot, ramp, steps, sums, send_main, got_main, send_edge, got_edge,
           load_sem, row_send, row_recv, main_send, main_recv, edge_send, edge_recv):
    chan = lax.axis_index("chan")
    tile = lax.axis_index("tile")
    chips_y = chans // NEAR
    at_y, at_x, at_core = chan // NEAR, lax.rem(chan // CORES, CHIPS_X), lax.rem(chan, CORES)
    next_tile, prev_tile = lax.rem(tile + 1, tiles), lax.rem(tile + tiles - 1, tiles)
    width = chans * LANES
    coarse = chans * COLS
    blocks = tile_ref.shape[0]

    one, nil = jnp.bfloat16(1), jnp.bfloat16(0)
    barrier = pltpu.get_barrier_semaphore()
    for step in reversed(near_first(tiles)[1:]):
        pl.semaphore_signal(barrier, inc=1, device_id={"tile": lax.rem(tile + step, tiles)}, device_id_type=MESH)
    for k in range(1, chans):
        other = lax.rem(chan + k, chans)
        pl.semaphore_signal(barrier, inc=1, device_id={"chan": other}, device_id_type=MESH)
        for z in (next_tile, prev_tile):
            pl.semaphore_signal(barrier, inc=1, device_id={"chan": other, "tile": z}, device_id_type=MESH)
    loads = [
        pltpu.make_async_copy(source, target, load_sem.at[at])
        for at, (source, target) in enumerate(
            [(tile_hbm, tile_ref), (cell_hbm, cell_ref), (plane_hbm, plane_ref),
             (offset_hbm, offset_ref), (vis_hbm, vis_ref), (table_hbm, table)]
        )
    ]
    for load in loads:
        load.start()

    loads[0].wait()
    owner = tile_ref[...]
    marks = jnp.concatenate([jnp.where(owner == t, 1.0, 0.0) for t in range(tiles)], axis=0)
    size = tiles * blocks
    marks16 = marks.astype(jnp.bfloat16)
    before = ones_where(iota((LANES, LANES), 0) < iota((LANES, LANES), 1))
    inside = jnp.dot(marks16, before, preferred_element_type=jnp.float32)
    totals = jnp.dot(marks16, jnp.ones((LANES, LANES), jnp.bfloat16), preferred_element_type=jnp.float32)
    here, there = iota((size, size), 0), iota((size, size), 1)
    earlier = ones_where((here // blocks == there // blocks) & (there < here))
    ahead = jnp.dot(earlier, totals.astype(jnp.bfloat16), preferred_element_type=jnp.float32)
    ranks[...] = jnp.where(marks > 0.5, inside + ahead, -1.0)

    for load in loads[1:5]:
        load.wait()
    cell = cell_ref[...]
    vis = vis_ref[...]
    high = vis.astype(jnp.bfloat16).astype(jnp.float32)
    rows[0:2, :] = high
    rows[2:4, :] = vis - high
    for at, field in enumerate([plane_ref[...], offset_ref[...], cell // 256, cell & 255]):
        field = field.astype(jnp.float32)
        for b in range(blocks):
            rows[4 + at : 5 + at, b * LANES : (b + 1) * LANES] = field[b : b + 1, :]
    rows16 = rows[...].astype(jnp.bfloat16)

    slot = iota((CAPACITY, LANES), 0).astype(jnp.float32)
    for t in range(tiles):
        pick = jnp.concatenate(
            [ones_where(slot == ranks[t * blocks + b : t * blocks + b + 1, :]) for b in range(blocks)], axis=1)
        send_rows[t] = lax.dot_general(rows16, pick, NT, preferred_element_type=jnp.float32).astype(jnp.bfloat16)

    loads[5].wait()
    highs = table.shape[0] // LOW
    for h in range(highs):
        lookup[h * LANES : (h + 1) * LANES, :] = table[h * LOW : (h + 1) * LOW, :].T

    shifted = iota((LOW, LANES), 0).astype(jnp.float32) - LOW // 2
    ramp[...] = shifted.astype(jnp.bfloat16)
    coarse_ramp = iota((coarse, LANES), 0).astype(jnp.float32) - coarse // 2
    steps[...] = coarse_ramp.astype(jnp.bfloat16)

    def hot(reference, value, count):
        value = value.astype(jnp.float32).astype(jnp.bfloat16)
        return jnp.concatenate(
            [jnp.where(reference == value[:, n * LANES : (n + 1) * LANES], one, nil) for n in range(count)], axis=1)

    def spread_rows(blocks_in, chunk):
        count = len(blocks_in)
        got = jnp.concatenate([block.astype(jnp.float32) for block in blocks_in], axis=1)
        real, imag = got[0:1] + got[2:3], got[1:2] + got[3:4]
        whole = got.astype(jnp.int32)
        plane, offset = whole[4:5], whole[5:6]
        cell = whole[6:7] * 256 + whole[7:8]
        u, v = cell & (width - 1), cell // width
        pick = hot(ramp[...], (plane & 7) * 64 + offset - LOW // 2, count)
        found = jnp.dot(lookup[...], pick, preferred_element_type=jnp.float32)
        kern = found[0:LANES]
        for h in range(1, highs):
            kern = jnp.where(plane // 8 == h, found[h * LANES : (h + 1) * LANES], kern)
        kern_real, kern_imag = kern[:AREA], kern[AREA:]
        parts = [real * kern_real - imag * kern_imag, real * kern_imag + imag * kern_real]

        onehot[:, :chunk] = hot(steps[...], u // SUPPORT - coarse // 2, count)
        onehot[:, chunk : 2 * chunk] = hot(steps[...], u // SUPPORT + 1 - coarse // 2, count)
        fine = u & (SUPPORT - 1)
        row = iota((SUPPORT, chunk), 0)
        turn = (row - v) & (SUPPORT - 1)
        taps = []
        for i in range(SUPPORT):
            pair = [turned(part[8 * i : 8 * i + 8], v, turn) for part in parts]
            taps.append(jnp.concatenate(pair, axis=0).astype(jnp.bfloat16))
        zero = jnp.zeros((2 * SUPPORT, chunk), jnp.bfloat16)
        for bit in range(3):
            by = 1 << bit
            flag = jnp.where((jnp.broadcast_to(fine, (2 * SUPPORT, chunk)) & by) != 0, 1.0, 0.0)
            on = flag.astype(jnp.bfloat16) > nil
            later = [zero] * by + taps
            kept = taps + [zero] * by
            taps = [jnp.where(on, x, y) for x, y in zip(later, kept)]
        taps = taps + [zero]
        keep = []
        for k in range(3):
            inside = jnp.where((row + 8 * k >= v) & (row + 8 * k < v + SUPPORT), 1.0, 0.0)
            keep.append(jnp.concatenate([inside, inside], axis=0).astype(jnp.bfloat16))
        for f in range(2 * SUPPORT):
            lanes, place = pl.ds(f // SUPPORT * chunk, chunk), f % SUPPORT
            for k in range(3):
                at = place * 2 * TILE_V + k * 2 * SUPPORT if k < 2 else MAIN + place * 2 * SUPPORT
                spread[at : at + 2 * SUPPORT, lanes] = taps[f] * keep[k]

    spread_rows([send_rows[tile]], CAPACITY)
    sums[...] = lax.dot_general(
        onehot[:, : 2 * CAPACITY], spread[:, : 2 * CAPACITY], NT, preferred_element_type=jnp.float32)

    pl.semaphore_wait(barrier, tiles - 1 + 3 * (chans - 1))
    order = near_first(tiles)
    row_copies = {}
    for j in reversed(range(1, tiles)):
        to = lax.rem(tile + order[j], tiles)
        row_copies[j] = pltpu.make_async_remote_copy(
            src_ref=send_rows.at[to], dst_ref=got_rows.at[j], send_sem=row_send.at[j], recv_sem=row_recv.at[j],
            device_id={"tile": to}, device_id_type=MESH)
        row_copies[j].start()

    main_copies, edge_copies = [], []
    for first, end in groups_of(tiles)[1:]:
        chunk = (end - first) * CAPACITY
        for j in range(first, end):
            row_copies[j].wait_recv()
        spread_rows([got_rows[j] for j in range(first, end)], chunk)
        taps_on = spread[:, : 2 * chunk]
        if end < tiles:
            add = lax.dot_general(onehot[:, : 2 * chunk], taps_on, NT, preferred_element_type=jnp.float32)
            sums[...] = sums[...] + add
            continue
        for dy in reversed(near_first(chips_y)):
            to_y = lax.rem(at_y + dy, chips_y)
            window = pl.ds(pl.multiple_of(to_y * BLOCK, BLOCK), BLOCK)
            piece = sums[window, :] + lax.dot_general(
                onehot[window, : 2 * chunk], taps_on, NT, preferred_element_type=jnp.float32)
            piece = piece.astype(jnp.bfloat16)
            for k in range(NEAR):
                send_main[to_y * NEAR + k] = piece[k * COLS : (k + 1) * COLS, :MAIN]
                send_edge[to_y * NEAR + k] = piece[k * COLS : (k + 1) * COLS, MAIN:]
            edges = []
            for dx in reversed(near_first(CHIPS_X)):
                for dc in range(CORES):
                    k = dy * NEAR + dx * CORES + dc
                    to = to_y * NEAR + lax.rem(at_x + dx, CHIPS_X) * CORES + lax.rem(at_core + dc, CORES)
                    edges.append(pltpu.make_async_remote_copy(
                        src_ref=send_edge.at[to], dst_ref=got_edge.at[k], send_sem=edge_send.at[k],
                        recv_sem=edge_recv.at[k], device_id={"chan": to, "tile": next_tile}, device_id_type=MESH))
                    if k > 0:
                        main_copies.append(pltpu.make_async_remote_copy(
                            src_ref=send_main.at[to], dst_ref=got_main.at[k], send_sem=main_send.at[k],
                            recv_sem=main_recv.at[k], device_id={"chan": to}, device_id_type=MESH))
                        main_copies[-1].start()
            edge_copies += edges

            @pl.when(tile < tiles - 1)
            def _():
                for copy in edges:
                    copy.start()

    got_main[0] = send_main[chan]
    for copy in main_copies:
        copy.wait_recv()

    @pl.when(tile > 0)
    def _():
        for copy in edge_copies:
            copy.wait_recv()

    main, past = got_main[0].astype(jnp.float32), got_edge[0].astype(jnp.float32)
    for k in range(1, chans):
        main = main + got_main[k].astype(jnp.float32)
        past = past + got_edge[k].astype(jnp.float32)
    past = jnp.where(tile > 0, past, 0.0)

    main, past = main.T, past.T
    strips = []
    for f in range(SUPPORT):
        own = main[f * 2 * TILE_V : (f + 1) * 2 * TILE_V]
        edge = past[f * 2 * SUPPORT : (f + 1) * 2 * SUPPORT]
        low = own[: 2 * SUPPORT] + edge
        high = own[2 * SUPPORT :]
        strips.append(jnp.concatenate([low[:8], high[:8], low[8:], high[8:]], axis=0))
    mixed = jnp.concatenate(strips, axis=1)
    source, target = iota((LANES, LANES), 0), iota((LANES, LANES), 1)
    place = ones_where(target == (source & (COLS - 1)) * SUPPORT + source // COLS)
    grid = jnp.zeros((2 * TILE_V, LANES), jnp.float32)
    for _ in range(3):
        term = mixed.astype(jnp.bfloat16)
        grid = grid + jnp.dot(term, place, preferred_element_type=jnp.float32)
        mixed = mixed - term.astype(jnp.float32)
    for c in range(2):
        out_ref[c] = grid[c * TILE_V : (c + 1) * TILE_V]
    for copy in list(row_copies.values()) + main_copies:
        copy.wait_send()

    @pl.when(tile < tiles - 1)
    def _():
        for copy in edge_copies:
            copy.wait_send()


def body(visibility, kernel_table, cell_index, tile_index, plane_index, offset_index):
    chans, tiles = lax.axis_size("chan"), lax.axis_size("tile")
    count = cell_index.shape[0]
    blocks = count // LANES
    shape = (blocks, LANES)
    coarse = chans * COLS
    chunk = WIDEST * CAPACITY
    return pl.pallas_call(
        functools.partial(kernel, chans, tiles),
        out_shape=jax.ShapeDtypeStruct((2, TILE_V, LANES), jnp.float32),
        in_specs=[pl.BlockSpec(memory_space=pltpu.HBM)] * 6,
        out_specs=pl.BlockSpec(memory_space=pltpu.VMEM),
        scratch_shapes=[
            pltpu.VMEM((2, count), jnp.float32),
            pltpu.VMEM(shape, jnp.int32),
            pltpu.VMEM(shape, jnp.int32),
            pltpu.VMEM(shape, jnp.int32),
            pltpu.VMEM(shape, jnp.int32),
            pltpu.VMEM(kernel_table.shape, kernel_table.dtype),
            pltpu.VMEM((FIELDS, count), jnp.float32),
            pltpu.VMEM((tiles * blocks, LANES), jnp.float32),
            pltpu.VMEM((kernel_table.shape[0] // LOW * LANES, LOW), jnp.bfloat16),
            pltpu.VMEM((tiles, FIELDS, CAPACITY), jnp.bfloat16),
            pltpu.VMEM((tiles, FIELDS, CAPACITY), jnp.bfloat16),
            pltpu.VMEM((HALF, 2 * chunk), jnp.bfloat16),
            pltpu.VMEM((coarse, 2 * chunk), jnp.bfloat16),
            pltpu.VMEM((LOW, LANES), jnp.bfloat16),
            pltpu.VMEM((coarse, LANES), jnp.bfloat16),
            pltpu.VMEM((coarse, HALF), jnp.float32),
            pltpu.VMEM((chans, COLS, MAIN), jnp.bfloat16),
            pltpu.VMEM((chans, COLS, MAIN), jnp.bfloat16),
            pltpu.VMEM((chans, COLS, EDGE), jnp.bfloat16),
            pltpu.VMEM((chans, COLS, EDGE), jnp.bfloat16),
            pltpu.SemaphoreType.DMA((6,)),
            pltpu.SemaphoreType.DMA((tiles,)),
            pltpu.SemaphoreType.DMA((tiles,)),
            pltpu.SemaphoreType.DMA((chans,)),
            pltpu.SemaphoreType.DMA((chans,)),
            pltpu.SemaphoreType.DMA((chans,)),
            pltpu.SemaphoreType.DMA((chans,)),
        ],
        compiler_params=pltpu.CompilerParams(
            collective_id=0, has_side_effects=True, vmem_limit_bytes=60 * 1024 * 1024),
    )(visibility, cell_index.reshape(shape), tile_index.reshape(shape), plane_index.reshape(shape),
      offset_index.reshape(shape), kernel_table)


def solution(mesh):
    placed = (
        P(None, ("chan", "tile")),
        P(),
        P(("chan", "tile")),
        P(("chan", "tile"), None),
        P(("chan", "tile")),
        P(("chan", "tile")),
    )
    return jax.shard_map(
        body, mesh=mesh, in_specs=placed, out_specs=P(None, "tile", "chan"), check_vma=False
    )
```

```python
import functools

import jax
import jax.numpy as jnp
from jax import lax
from jax.experimental import pallas as pl
from jax.experimental.pallas import tpu as pltpu
from jax.sharding import PartitionSpec as P

SUPPORT = 8
TILE_V = 16
CAPACITY = 128
LANES = 128
AREA = SUPPORT * SUPPORT
FIELDS = 8
LOW = 512
WIDEST = 4
COLS = LANES // SUPPORT
MAIN = SUPPORT * 2 * TILE_V
EDGE = SUPPORT * 2 * SUPPORT
HALF = MAIN + EDGE
CHIPS_X = 4
CORES = 2
NEAR = CHIPS_X * CORES
BLOCK = NEAR * COLS
MESH = pl.DeviceIdType.MESH
NT = (((1,), (1,)), ((), ()))


def iota(shape, axis):
    return lax.broadcasted_iota(jnp.int32, shape, axis)


def ones_where(mask):
    return jnp.where(mask, 1.0, 0.0).astype(jnp.bfloat16)


def groups_of(tiles):
    bounds = [0] + list(range(1, tiles, WIDEST)) + [tiles]
    return list(zip(bounds[:-1], bounds[1:]))


def turned(tap, v, turn):
    return jnp.take_along_axis(tap, turn, axis=0, mode="promise_in_bounds")


def near_first(size):
    return sorted(range(size), key=lambda step: min(step, size - step))


def kernel(chans, tiles, vis_hbm, cell_hbm, tile_hbm, plane_hbm, offset_hbm, table_hbm, out_ref,
           vis_ref, cell_ref, tile_ref, plane_ref, offset_ref, table, rows, ranks, lookup,
           send_rows, got_rows, spread, onehot, ramp, steps, sums, send_main, got_main, send_edge, got_edge,
           load_sem, row_send, row_recv, main_send, main_recv, edge_send, edge_recv):
    chan = lax.axis_index("chan")
    tile = lax.axis_index("tile")
    chips_y = chans // NEAR
    at_y, at_x, at_core = chan // NEAR, lax.rem(chan // CORES, CHIPS_X), lax.rem(chan, CORES)
    next_tile, prev_tile = lax.rem(tile + 1, tiles), lax.rem(tile + tiles - 1, tiles)
    width = chans * LANES
    coarse = chans * COLS
    blocks = tile_ref.shape[0]

    one, nil = jnp.bfloat16(1), jnp.bfloat16(0)
    barrier = pltpu.get_barrier_semaphore()
    for step in reversed(near_first(tiles)[1:]):
        pl.semaphore_signal(barrier, inc=1, device_id={"tile": lax.rem(tile + step, tiles)}, device_id_type=MESH)
    loads = [
        pltpu.make_async_copy(source, target, load_sem.at[at])
        for at, (source, target) in enumerate(
            [(tile_hbm, tile_ref), (cell_hbm, cell_ref), (plane_hbm, plane_ref),
             (offset_hbm, offset_ref), (vis_hbm, vis_ref), (table_hbm, table)]
        )
    ]
    for load in loads:
        load.start()
    for k in range(1, chans):
        other = lax.rem(chan + k, chans)
        pl.semaphore_signal(barrier, inc=1, device_id={"chan": other}, device_id_type=MESH)
        for z in (next_tile, prev_tile):
            pl.semaphore_signal(barrier, inc=1, device_id={"chan": other, "tile": z}, device_id_type=MESH)

    loads[0].wait()
    owner = tile_ref[...]
    marks = jnp.concatenate([jnp.where(owner == t, 1.0, 0.0) for t in range(tiles)], axis=0)
    size = tiles * blocks
    marks16 = marks.astype(jnp.bfloat16)
    before = ones_where(iota((LANES, LANES), 0) < iota((LANES, LANES), 1))
    inside = jnp.dot(marks16, before, preferred_element_type=jnp.float32)
    totals = jnp.dot(marks16, jnp.ones((LANES, LANES), jnp.bfloat16), preferred_element_type=jnp.float32)
    here, there = iota((size, size), 0), iota((size, size), 1)
    earlier = ones_where((here // blocks == there // blocks) & (there < here))
    ahead = jnp.dot(earlier, totals.astype(jnp.bfloat16), preferred_element_type=jnp.float32)
    ranks[...] = jnp.where(marks > 0.5, inside + ahead, -1.0)

    for load in loads[1:5]:
        load.wait()
    cell = cell_ref[...]
    vis = vis_ref[...]
    high = vis.astype(jnp.bfloat16).astype(jnp.float32)
    rows[0:2, :] = high
    rows[2:4, :] = vis - high
    for at, field in enumerate([plane_ref[...], offset_ref[...], cell // 256, cell & 255]):
        field = field.astype(jnp.float32)
        for b in range(blocks):
            rows[4 + at : 5 + at, b * LANES : (b + 1) * LANES] = field[b : b + 1, :]
    rows16 = rows[...].astype(jnp.bfloat16)

    slot = iota((CAPACITY, LANES), 0).astype(jnp.float32)
    for t in range(tiles):
        pick = jnp.concatenate(
            [ones_where(slot == ranks[t * blocks + b : t * blocks + b + 1, :]) for b in range(blocks)], axis=1)
        send_rows[t] = lax.dot_general(rows16, pick, NT, preferred_element_type=jnp.float32).astype(jnp.bfloat16)

    loads[5].wait()
    highs = table.shape[0] // LOW
    for h in range(highs):
        lookup[h * LANES : (h + 1) * LANES, :] = table[h * LOW : (h + 1) * LOW, :].T

    shifted = iota((LOW, LANES), 0).astype(jnp.float32) - LOW // 2
    ramp[...] = shifted.astype(jnp.bfloat16)
    coarse_ramp = iota((coarse, LANES), 0).astype(jnp.float32) - coarse // 2
    steps[...] = coarse_ramp.astype(jnp.bfloat16)

    def hot(reference, value, count):
        value = value.astype(jnp.float32).astype(jnp.bfloat16)
        return jnp.concatenate(
            [jnp.where(reference == value[:, n * LANES : (n + 1) * LANES], one, nil) for n in range(count)], axis=1)

    def spread_rows(blocks_in, chunk):
        count = len(blocks_in)
        got = jnp.concatenate([block.astype(jnp.float32) for block in blocks_in], axis=1)
        real, imag = got[0:1] + got[2:3], got[1:2] + got[3:4]
        whole = got.astype(jnp.int32)
        plane, offset = whole[4:5], whole[5:6]
        cell = whole[6:7] * 256 + whole[7:8]
        u, v = cell & (width - 1), cell // width
        pick = hot(ramp[...], (plane & 7) * 64 + offset - LOW // 2, count)
        found = jnp.dot(lookup[...], pick, preferred_element_type=jnp.float32)
        kern = found[0:LANES]
        for h in range(1, highs):
            kern = jnp.where(plane // 8 == h, found[h * LANES : (h + 1) * LANES], kern)
        kern_real, kern_imag = kern[:AREA], kern[AREA:]
        parts = [real * kern_real - imag * kern_imag, real * kern_imag + imag * kern_real]

        onehot[:, :chunk] = hot(steps[...], u // SUPPORT - coarse // 2, count)
        onehot[:, chunk : 2 * chunk] = hot(steps[...], u // SUPPORT + 1 - coarse // 2, count)
        fine = u & (SUPPORT - 1)
        row = iota((SUPPORT, chunk), 0)
        turn = (row - v) & (SUPPORT - 1)
        taps = []
        for i in range(SUPPORT):
            pair = [turned(part[8 * i : 8 * i + 8], v, turn) for part in parts]
            taps.append(jnp.concatenate(pair, axis=0).astype(jnp.bfloat16))
        zero = jnp.zeros((2 * SUPPORT, chunk), jnp.bfloat16)
        for bit in range(3):
            by = 1 << bit
            flag = jnp.where((jnp.broadcast_to(fine, (2 * SUPPORT, chunk)) & by) != 0, 1.0, 0.0)
            on = flag.astype(jnp.bfloat16) > nil
            later = [zero] * by + taps
            kept = taps + [zero] * by
            taps = [jnp.where(on, x, y) for x, y in zip(later, kept)]
        taps = taps + [zero]
        keep = []
        for k in range(3):
            inside = jnp.where((row + 8 * k >= v) & (row + 8 * k < v + SUPPORT), 1.0, 0.0)
            keep.append(jnp.concatenate([inside, inside], axis=0).astype(jnp.bfloat16))
        for f in range(2 * SUPPORT):
            lanes, place = pl.ds(f // SUPPORT * chunk, chunk), f % SUPPORT
            for k in range(3):
                at = place * 2 * TILE_V + k * 2 * SUPPORT if k < 2 else MAIN + place * 2 * SUPPORT
                spread[at : at + 2 * SUPPORT, lanes] = taps[f] * keep[k]

    spread_rows([send_rows[tile]], CAPACITY)
    sums[...] = lax.dot_general(
        onehot[:, : 2 * CAPACITY], spread[:, : 2 * CAPACITY], NT, preferred_element_type=jnp.float32)

    pl.semaphore_wait(barrier, tiles - 1 + 3 * (chans - 1))
    order = near_first(tiles)
    row_copies = {}
    for j in range(1, tiles):
        to = lax.rem(tile + order[j], tiles)
        row_copies[j] = pltpu.make_async_remote_copy(
            src_ref=send_rows.at[to], dst_ref=got_rows.at[j], send_sem=row_send.at[j], recv_sem=row_recv.at[j],
            device_id={"tile": to}, device_id_type=MESH)
        row_copies[j].start()

    main_copies, edge_copies = [], []
    for first, end in groups_of(tiles)[1:]:
        chunk = (end - first) * CAPACITY
        for j in range(first, end):
            row_copies[j].wait_recv()
        spread_rows([got_rows[j] for j in range(first, end)], chunk)
        taps_on = spread[:, : 2 * chunk]
        if end < tiles:
            add = lax.dot_general(onehot[:, : 2 * chunk], taps_on, NT, preferred_element_type=jnp.float32)
            sums[...] = sums[...] + add
            continue
        for dy in reversed(near_first(chips_y)):
            to_y = lax.rem(at_y + dy, chips_y)
            window = pl.ds(pl.multiple_of(to_y * BLOCK, BLOCK), BLOCK)
            piece = sums[window, :] + lax.dot_general(
                onehot[window, : 2 * chunk], taps_on, NT, preferred_element_type=jnp.float32)
            piece = piece.astype(jnp.bfloat16)
            for k in range(NEAR):
                send_main[to_y * NEAR + k] = piece[k * COLS : (k + 1) * COLS, :MAIN]
                send_edge[to_y * NEAR + k] = piece[k * COLS : (k + 1) * COLS, MAIN:]
            edges = []
            for dx in reversed(near_first(CHIPS_X)):
                for dc in range(CORES):
                    k = dy * NEAR + dx * CORES + dc
                    to = to_y * NEAR + lax.rem(at_x + dx, CHIPS_X) * CORES + lax.rem(at_core + dc, CORES)
                    edges.append(pltpu.make_async_remote_copy(
                        src_ref=send_edge.at[to], dst_ref=got_edge.at[k], send_sem=edge_send.at[k],
                        recv_sem=edge_recv.at[k], device_id={"chan": to, "tile": next_tile}, device_id_type=MESH))
                    if k > 0:
                        main_copies.append(pltpu.make_async_remote_copy(
                            src_ref=send_main.at[to], dst_ref=got_main.at[k], send_sem=main_send.at[k],
                            recv_sem=main_recv.at[k], device_id={"chan": to}, device_id_type=MESH))
                        main_copies[-1].start()
            edge_copies += edges

    @pl.when(tile < tiles - 1)
    def _():
        for copy in edge_copies:
            copy.start()

    got_main[0] = send_main[chan]
    for copy in main_copies:
        copy.wait_recv()

    @pl.when(tile > 0)
    def _():
        for copy in edge_copies:
            copy.wait_recv()

    main, past = got_main[0].astype(jnp.float32), got_edge[0].astype(jnp.float32)
    for k in range(1, chans):
        main = main + got_main[k].astype(jnp.float32)
        past = past + got_edge[k].astype(jnp.float32)
    past = jnp.where(tile > 0, past, 0.0)

    main, past = main.T, past.T
    strips = []
    for f in range(SUPPORT):
        own = main[f * 2 * TILE_V : (f + 1) * 2 * TILE_V]
        edge = past[f * 2 * SUPPORT : (f + 1) * 2 * SUPPORT]
        low = own[: 2 * SUPPORT] + edge
        high = own[2 * SUPPORT :]
        strips.append(jnp.concatenate([low[:8], high[:8], low[8:], high[8:]], axis=0))
    mixed = jnp.concatenate(strips, axis=1)
    source, target = iota((LANES, LANES), 0), iota((LANES, LANES), 1)
    place = ones_where(target == (source & (COLS - 1)) * SUPPORT + source // COLS)
    grid = jnp.zeros((2 * TILE_V, LANES), jnp.float32)
    for _ in range(3):
        term = mixed.astype(jnp.bfloat16)
        grid = grid + jnp.dot(term, place, preferred_element_type=jnp.float32)
        mixed = mixed - term.astype(jnp.float32)
    for c in range(2):
        out_ref[c] = grid[c * TILE_V : (c + 1) * TILE_V]
    for copy in list(row_copies.values()) + main_copies:
        copy.wait_send()

    @pl.when(tile < tiles - 1)
    def _():
        for copy in edge_copies:
            copy.wait_send()


def body(visibility, kernel_table, cell_index, tile_index, plane_index, offset_index):
    chans, tiles = lax.axis_size("chan"), lax.axis_size("tile")
    count = cell_index.shape[0]
    blocks = count // LANES
    shape = (blocks, LANES)
    coarse = chans * COLS
    chunk = WIDEST * CAPACITY
    return pl.pallas_call(
        functools.partial(kernel, chans, tiles),
        out_shape=jax.ShapeDtypeStruct((2, TILE_V, LANES), jnp.float32),
        in_specs=[pl.BlockSpec(memory_space=pltpu.HBM)] * 6,
        out_specs=pl.BlockSpec(memory_space=pltpu.VMEM),
        scratch_shapes=[
            pltpu.VMEM((2, count), jnp.float32),
            pltpu.VMEM(shape, jnp.int32),
            pltpu.VMEM(shape, jnp.int32),
            pltpu.VMEM(shape, jnp.int32),
            pltpu.VMEM(shape, jnp.int32),
            pltpu.VMEM(kernel_table.shape, kernel_table.dtype),
            pltpu.VMEM((FIELDS, count), jnp.float32),
            pltpu.VMEM((tiles * blocks, LANES), jnp.float32),
            pltpu.VMEM((kernel_table.shape[0] // LOW * LANES, LOW), jnp.bfloat16),
            pltpu.VMEM((tiles, FIELDS, CAPACITY), jnp.bfloat16),
            pltpu.VMEM((tiles, FIELDS, CAPACITY), jnp.bfloat16),
            pltpu.VMEM((HALF, 2 * chunk), jnp.bfloat16),
            pltpu.VMEM((coarse, 2 * chunk), jnp.bfloat16),
            pltpu.VMEM((LOW, LANES), jnp.bfloat16),
            pltpu.VMEM((coarse, LANES), jnp.bfloat16),
            pltpu.VMEM((coarse, HALF), jnp.float32),
            pltpu.VMEM((chans, COLS, MAIN), jnp.bfloat16),
            pltpu.VMEM((chans, COLS, MAIN), jnp.bfloat16),
            pltpu.VMEM((chans, COLS, EDGE), jnp.bfloat16),
            pltpu.VMEM((chans, COLS, EDGE), jnp.bfloat16),
            pltpu.SemaphoreType.DMA((6,)),
            pltpu.SemaphoreType.DMA((tiles,)),
            pltpu.SemaphoreType.DMA((tiles,)),
            pltpu.SemaphoreType.DMA((chans,)),
            pltpu.SemaphoreType.DMA((chans,)),
            pltpu.SemaphoreType.DMA((chans,)),
            pltpu.SemaphoreType.DMA((chans,)),
        ],
        compiler_params=pltpu.CompilerParams(
            collective_id=0, has_side_effects=True, vmem_limit_bytes=60 * 1024 * 1024),
    )(visibility, cell_index.reshape(shape), tile_index.reshape(shape), plane_index.reshape(shape),
      offset_index.reshape(shape), kernel_table)


def solution(mesh):
    placed = (
        P(None, ("chan", "tile")),
        P(),
        P(("chan", "tile")),
        P(("chan", "tile"), None),
        P(("chan", "tile")),
        P(("chan", "tile")),
    )
    return jax.shard_map(
        body, mesh=mesh, in_specs=placed, out_specs=P(None, "tile", "chan"), check_vma=False
    )
```

```python
import functools

import jax
import jax.numpy as jnp
from jax import lax
from jax.experimental import pallas as pl
from jax.experimental.pallas import tpu as pltpu
from jax.sharding import PartitionSpec as P

SUPPORT = 8
TILE_V = 16
CAPACITY = 128
LANES = 128
AREA = SUPPORT * SUPPORT
FIELDS = 8
LOW = 512
WIDEST = 6
COLS = LANES // SUPPORT
MAIN = SUPPORT * 2 * TILE_V
EDGE = SUPPORT * 2 * SUPPORT
HALF = MAIN + EDGE
CHIPS_X = 4
CORES = 2
NEAR = CHIPS_X * CORES
BLOCK = NEAR * COLS
MESH = pl.DeviceIdType.MESH
NT = (((1,), (1,)), ((), ()))


def iota(shape, axis):
    return lax.broadcasted_iota(jnp.int32, shape, axis)


def ones_where(mask):
    return jnp.where(mask, 1.0, 0.0).astype(jnp.bfloat16)


def groups_of(tiles):
    bounds = [0] + list(range(1, tiles, WIDEST)) + [tiles]
    return list(zip(bounds[:-1], bounds[1:]))


def turned(tap, v, turn):
    return jnp.take_along_axis(tap, turn, axis=0, mode="promise_in_bounds")


def near_first(size):
    return sorted(range(size), key=lambda step: min(step, size - step))


def kernel(chans, tiles, vis_hbm, cell_hbm, tile_hbm, plane_hbm, offset_hbm, table_hbm, out_ref,
           vis_ref, cell_ref, tile_ref, plane_ref, offset_ref, table, rows, ranks, lookup,
           send_rows, got_rows, spread, onehot, ramp, steps, sums, send_main, got_main, send_edge, got_edge,
           load_sem, row_send, row_recv, main_send, main_recv, edge_send, edge_recv):
    chan = lax.axis_index("chan")
    tile = lax.axis_index("tile")
    chips_y = chans // NEAR
    at_y, at_x, at_core = chan // NEAR, lax.rem(chan // CORES, CHIPS_X), lax.rem(chan, CORES)
    next_tile, prev_tile = lax.rem(tile + 1, tiles), lax.rem(tile + tiles - 1, tiles)
    width = chans * LANES
    coarse = chans * COLS
    blocks = tile_ref.shape[0]

    one, nil = jnp.bfloat16(1), jnp.bfloat16(0)
    barrier = pltpu.get_barrier_semaphore()
    for step in reversed(near_first(tiles)[1:]):
        pl.semaphore_signal(barrier, inc=1, device_id={"tile": lax.rem(tile + step, tiles)}, device_id_type=MESH)
    loads = [
        pltpu.make_async_copy(source, target, load_sem.at[at])
        for at, (source, target) in enumerate(
            [(tile_hbm, tile_ref), (cell_hbm, cell_ref), (plane_hbm, plane_ref),
             (offset_hbm, offset_ref), (vis_hbm, vis_ref), (table_hbm, table)]
        )
    ]
    for load in loads:
        load.start()
    for k in range(1, chans):
        other = lax.rem(chan + k, chans)
        pl.semaphore_signal(barrier, inc=1, device_id={"chan": other}, device_id_type=MESH)
        for z in (next_tile, prev_tile):
            pl.semaphore_signal(barrier, inc=1, device_id={"chan": other, "tile": z}, device_id_type=MESH)

    loads[0].wait()
    owner = tile_ref[...]
    marks = jnp.concatenate([jnp.where(owner == t, 1.0, 0.0) for t in range(tiles)], axis=0)
    size = tiles * blocks
    marks16 = marks.astype(jnp.bfloat16)
    before = ones_where(iota((LANES, LANES), 0) < iota((LANES, LANES), 1))
    inside = jnp.dot(marks16, before, preferred_element_type=jnp.float32)
    totals = jnp.dot(marks16, jnp.ones((LANES, LANES), jnp.bfloat16), preferred_element_type=jnp.float32)
    here, there = iota((size, size), 0), iota((size, size), 1)
    earlier = ones_where((here // blocks == there // blocks) & (there < here))
    ahead = jnp.dot(earlier, totals.astype(jnp.bfloat16), preferred_element_type=jnp.float32)
    ranks[...] = jnp.where(marks > 0.5, inside + ahead, -1.0)

    for load in loads[1:5]:
        load.wait()
    cell = cell_ref[...]
    vis = vis_ref[...]
    high = vis.astype(jnp.bfloat16).astype(jnp.float32)
    rows[0:2, :] = high
    rows[2:4, :] = vis - high
    for at, field in enumerate([plane_ref[...], offset_ref[...], cell // 256, cell & 255]):
        field = field.astype(jnp.float32)
        for b in range(blocks):
            rows[4 + at : 5 + at, b * LANES : (b + 1) * LANES] = field[b : b + 1, :]
    rows16 = rows[...].astype(jnp.bfloat16)

    slot = iota((CAPACITY, LANES), 0).astype(jnp.float32)
    for t in range(tiles):
        pick = jnp.concatenate(
            [ones_where(slot == ranks[t * blocks + b : t * blocks + b + 1, :]) for b in range(blocks)], axis=1)
        send_rows[t] = lax.dot_general(rows16, pick, NT, preferred_element_type=jnp.float32).astype(jnp.bfloat16)

    loads[5].wait()
    highs = table.shape[0] // LOW
    for h in range(highs):
        lookup[h * LANES : (h + 1) * LANES, :] = table[h * LOW : (h + 1) * LOW, :].T

    shifted = iota((LOW, LANES), 0).astype(jnp.float32) - LOW // 2
    ramp[...] = shifted.astype(jnp.bfloat16)
    coarse_ramp = iota((coarse, LANES), 0).astype(jnp.float32) - coarse // 2
    steps[...] = coarse_ramp.astype(jnp.bfloat16)

    def hot(reference, value, count):
        value = value.astype(jnp.float32).astype(jnp.bfloat16)
        return jnp.concatenate(
            [jnp.where(reference == value[:, n * LANES : (n + 1) * LANES], one, nil) for n in range(count)], axis=1)

    def spread_rows(blocks_in, chunk):
        count = len(blocks_in)
        got = jnp.concatenate([block.astype(jnp.float32) for block in blocks_in], axis=1)
        real, imag = got[0:1] + got[2:3], got[1:2] + got[3:4]
        whole = got.astype(jnp.int32)
        plane, offset = whole[4:5], whole[5:6]
        cell = whole[6:7] * 256 + whole[7:8]
        u, v = cell & (width - 1), cell // width
        pick = hot(ramp[...], (plane & 7) * 64 + offset - LOW // 2, count)
        found = jnp.dot(lookup[...], pick, preferred_element_type=jnp.float32)
        kern = found[0:LANES]
        for h in range(1, highs):
            kern = jnp.where(plane // 8 == h, found[h * LANES : (h + 1) * LANES], kern)
        kern_real, kern_imag = kern[:AREA], kern[AREA:]
        parts = [real * kern_real - imag * kern_imag, real * kern_imag + imag * kern_real]

        onehot[:, :chunk] = hot(steps[...], u // SUPPORT - coarse // 2, count)
        onehot[:, chunk : 2 * chunk] = hot(steps[...], u // SUPPORT + 1 - coarse // 2, count)
        fine = u & (SUPPORT - 1)
        row = iota((SUPPORT, chunk), 0)
        turn = (row - v) & (SUPPORT - 1)
        taps = []
        for i in range(SUPPORT):
            pair = [turned(part[8 * i : 8 * i + 8], v, turn) for part in parts]
            taps.append(jnp.concatenate(pair, axis=0).astype(jnp.bfloat16))
        zero = jnp.zeros((2 * SUPPORT, chunk), jnp.bfloat16)
        for bit in range(3):
            by = 1 << bit
            flag = jnp.where((jnp.broadcast_to(fine, (2 * SUPPORT, chunk)) & by) != 0, 1.0, 0.0)
            on = flag.astype(jnp.bfloat16) > nil
            later = [zero] * by + taps
            kept = taps + [zero] * by
            taps = [jnp.where(on, x, y) for x, y in zip(later, kept)]
        taps = taps + [zero]
        keep = []
        for k in range(3):
            inside = jnp.where((row + 8 * k >= v) & (row + 8 * k < v + SUPPORT), 1.0, 0.0)
            keep.append(jnp.concatenate([inside, inside], axis=0).astype(jnp.bfloat16))
        for f in range(2 * SUPPORT):
            lanes, place = pl.ds(f // SUPPORT * chunk, chunk), f % SUPPORT
            for k in range(3):
                at = place * 2 * TILE_V + k * 2 * SUPPORT if k < 2 else MAIN + place * 2 * SUPPORT
                spread[at : at + 2 * SUPPORT, lanes] = taps[f] * keep[k]

    spread_rows([send_rows[tile]], CAPACITY)
    sums[...] = lax.dot_general(
        onehot[:, : 2 * CAPACITY], spread[:, : 2 * CAPACITY], NT, preferred_element_type=jnp.float32)

    pl.semaphore_wait(barrier, tiles - 1 + 3 * (chans - 1))
    order = near_first(tiles)
    row_copies = {}
    for j in range(1, tiles):
        to = lax.rem(tile + order[j], tiles)
        row_copies[j] = pltpu.make_async_remote_copy(
            src_ref=send_rows.at[to], dst_ref=got_rows.at[j], send_sem=row_send.at[j], recv_sem=row_recv.at[j],
            device_id={"tile": to}, device_id_type=MESH)
        row_copies[j].start()

    main_copies, main_slots, edge_copies = [], [], []
    for first, end in groups_of(tiles)[1:]:
        chunk = (end - first) * CAPACITY
        for j in range(first, end):
            row_copies[j].wait_recv()
        spread_rows([got_rows[j] for j in range(first, end)], chunk)
        taps_on = spread[:, : 2 * chunk]
        if end < tiles:
            add = lax.dot_general(onehot[:, : 2 * chunk], taps_on, NT, preferred_element_type=jnp.float32)
            sums[...] = sums[...] + add
            continue
        for dy in reversed(near_first(chips_y)):
            to_y = lax.rem(at_y + dy, chips_y)
            window = pl.ds(pl.multiple_of(to_y * BLOCK, BLOCK), BLOCK)
            piece = sums[window, :] + lax.dot_general(
                onehot[window, : 2 * chunk], taps_on, NT, preferred_element_type=jnp.float32)
            piece = piece.astype(jnp.bfloat16)
            for k in range(NEAR):
                send_main[to_y * NEAR + k] = piece[k * COLS : (k + 1) * COLS, :MAIN]
                send_edge[to_y * NEAR + k] = piece[k * COLS : (k + 1) * COLS, MAIN:]
            edges = []
            for dx in reversed(near_first(CHIPS_X)):
                for dc in range(CORES):
                    k = dy * NEAR + dx * CORES + dc
                    to = to_y * NEAR + lax.rem(at_x + dx, CHIPS_X) * CORES + lax.rem(at_core + dc, CORES)
                    edges.append(pltpu.make_async_remote_copy(
                        src_ref=send_edge.at[to], dst_ref=got_edge.at[k], send_sem=edge_send.at[k],
                        recv_sem=edge_recv.at[k], device_id={"chan": to, "tile": next_tile}, device_id_type=MESH))
                    if k > 0:
                        main_copies.append(pltpu.make_async_remote_copy(
                            src_ref=send_main.at[to], dst_ref=got_main.at[k], send_sem=main_send.at[k],
                            recv_sem=main_recv.at[k], device_id={"chan": to}, device_id_type=MESH))
                        main_copies[-1].start()
                        main_slots.append(k)
            edge_copies += edges

    @pl.when(tile < tiles - 1)
    def _():
        for copy in edge_copies:
            copy.start()

    got_main[0] = send_main[chan]
    main = got_main[0].astype(jnp.float32)
    for copy, k in zip(main_copies, main_slots):
        copy.wait_recv()
        main = main + got_main[k].astype(jnp.float32)

    @pl.when(tile > 0)
    def _():
        for copy in edge_copies:
            copy.wait_recv()

    past = got_edge[0].astype(jnp.float32)
    for k in range(1, chans):
        past = past + got_edge[k].astype(jnp.float32)
    past = jnp.where(tile > 0, past, 0.0)

    main, past = main.T, past.T
    strips = []
    for f in range(SUPPORT):
        own = main[f * 2 * TILE_V : (f + 1) * 2 * TILE_V]
        edge = past[f * 2 * SUPPORT : (f + 1) * 2 * SUPPORT]
        low = own[: 2 * SUPPORT] + edge
        high = own[2 * SUPPORT :]
        strips.append(jnp.concatenate([low[:8], high[:8], low[8:], high[8:]], axis=0))
    mixed = jnp.concatenate(strips, axis=1)
    source, target = iota((LANES, LANES), 0), iota((LANES, LANES), 1)
    place = ones_where(target == (source & (COLS - 1)) * SUPPORT + source // COLS)
    grid = jnp.zeros((2 * TILE_V, LANES), jnp.float32)
    for _ in range(3):
        term = mixed.astype(jnp.bfloat16)
        grid = grid + jnp.dot(term, place, preferred_element_type=jnp.float32)
        mixed = mixed - term.astype(jnp.float32)
    for c in range(2):
        out_ref[c] = grid[c * TILE_V : (c + 1) * TILE_V]
    for copy in list(row_copies.values()) + main_copies:
        copy.wait_send()

    @pl.when(tile < tiles - 1)
    def _():
        for copy in edge_copies:
            copy.wait_send()


def body(visibility, kernel_table, cell_index, tile_index, plane_index, offset_index):
    chans, tiles = lax.axis_size("chan"), lax.axis_size("tile")
    count = cell_index.shape[0]
    blocks = count // LANES
    shape = (blocks, LANES)
    coarse = chans * COLS
    chunk = WIDEST * CAPACITY
    return pl.pallas_call(
        functools.partial(kernel, chans, tiles),
        out_shape=jax.ShapeDtypeStruct((2, TILE_V, LANES), jnp.float32),
        in_specs=[pl.BlockSpec(memory_space=pltpu.HBM)] * 6,
        out_specs=pl.BlockSpec(memory_space=pltpu.VMEM),
        scratch_shapes=[
            pltpu.VMEM((2, count), jnp.float32),
            pltpu.VMEM(shape, jnp.int32),
            pltpu.VMEM(shape, jnp.int32),
            pltpu.VMEM(shape, jnp.int32),
            pltpu.VMEM(shape, jnp.int32),
            pltpu.VMEM(kernel_table.shape, kernel_table.dtype),
            pltpu.VMEM((FIELDS, count), jnp.float32),
            pltpu.VMEM((tiles * blocks, LANES), jnp.float32),
            pltpu.VMEM((kernel_table.shape[0] // LOW * LANES, LOW), jnp.bfloat16),
            pltpu.VMEM((tiles, FIELDS, CAPACITY), jnp.bfloat16),
            pltpu.VMEM((tiles, FIELDS, CAPACITY), jnp.bfloat16),
            pltpu.VMEM((HALF, 2 * chunk), jnp.bfloat16),
            pltpu.VMEM((coarse, 2 * chunk), jnp.bfloat16),
            pltpu.VMEM((LOW, LANES), jnp.bfloat16),
            pltpu.VMEM((coarse, LANES), jnp.bfloat16),
            pltpu.VMEM((coarse, HALF), jnp.float32),
            pltpu.VMEM((chans, COLS, MAIN), jnp.bfloat16),
            pltpu.VMEM((chans, COLS, MAIN), jnp.bfloat16),
            pltpu.VMEM((chans, COLS, EDGE), jnp.bfloat16),
            pltpu.VMEM((chans, COLS, EDGE), jnp.bfloat16),
            pltpu.SemaphoreType.DMA((6,)),
            pltpu.SemaphoreType.DMA((tiles,)),
            pltpu.SemaphoreType.DMA((tiles,)),
            pltpu.SemaphoreType.DMA((chans,)),
            pltpu.SemaphoreType.DMA((chans,)),
            pltpu.SemaphoreType.DMA((chans,)),
            pltpu.SemaphoreType.DMA((chans,)),
        ],
        compiler_params=pltpu.CompilerParams(
            collective_id=0, has_side_effects=True, vmem_limit_bytes=60 * 1024 * 1024),
    )(visibility, cell_index.reshape(shape), tile_index.reshape(shape), plane_index.reshape(shape),
      offset_index.reshape(shape), kernel_table)


def solution(mesh):
    placed = (
        P(None, ("chan", "tile")),
        P(),
        P(("chan", "tile")),
        P(("chan", "tile"), None),
        P(("chan", "tile")),
        P(("chan", "tile")),
    )
    return jax.shard_map(
        body, mesh=mesh, in_specs=placed, out_specs=P(None, "tile", "chan"), check_vma=False
    )
```

```python
import functools

import jax
import jax.numpy as jnp
from jax import lax
from jax.experimental import pallas as pl
from jax.experimental.pallas import tpu as pltpu
from jax.sharding import PartitionSpec as P

SUPPORT = 8
TILE_V = 16
CAPACITY = 128
LANES = 128
AREA = SUPPORT * SUPPORT
FIELDS = 8
LOW = 512
WIDEST = 7
COLS = LANES // SUPPORT
MAIN = SUPPORT * 2 * TILE_V
EDGE = SUPPORT * 2 * SUPPORT
HALF = MAIN + EDGE
CHIPS_X = 4
CORES = 2
NEAR = CHIPS_X * CORES
BLOCK = NEAR * COLS
MESH = pl.DeviceIdType.MESH
NT = (((1,), (1,)), ((), ()))


def iota(shape, axis):
    return lax.broadcasted_iota(jnp.int32, shape, axis)


def ones_where(mask):
    return jnp.where(mask, 1.0, 0.0).astype(jnp.bfloat16)


def groups_of(tiles):
    bounds = [0] + list(range(1, tiles, WIDEST)) + [tiles]
    return list(zip(bounds[:-1], bounds[1:]))


def turned(tap, v, turn):
    return jnp.take_along_axis(tap, turn, axis=0, mode="promise_in_bounds")


def near_first(size):
    return sorted(range(size), key=lambda step: min(step, size - step))


def kernel(chans, tiles, vis_hbm, cell_hbm, tile_hbm, plane_hbm, offset_hbm, table_hbm, out_ref,
           vis_ref, cell_ref, tile_ref, plane_ref, offset_ref, table, rows, ranks, lookup,
           send_rows, got_rows, spread, onehot, ramp, steps, sums, send_main, got_main, send_edge, got_edge,
           load_sem, row_send, row_recv, main_send, main_recv, edge_send, edge_recv):
    chan = lax.axis_index("chan")
    tile = lax.axis_index("tile")
    chips_y = chans // NEAR
    at_y, at_x, at_core = chan // NEAR, lax.rem(chan // CORES, CHIPS_X), lax.rem(chan, CORES)
    next_tile, prev_tile = lax.rem(tile + 1, tiles), lax.rem(tile + tiles - 1, tiles)
    width = chans * LANES
    coarse = chans * COLS
    blocks = tile_ref.shape[0]

    one, nil = jnp.bfloat16(1), jnp.bfloat16(0)
    barrier = pltpu.get_barrier_semaphore()
    for step in reversed(near_first(tiles)[1:]):
        pl.semaphore_signal(barrier, inc=1, device_id={"tile": lax.rem(tile + step, tiles)}, device_id_type=MESH)
    loads = [
        pltpu.make_async_copy(source, target, load_sem.at[at])
        for at, (source, target) in enumerate(
            [(tile_hbm, tile_ref), (cell_hbm, cell_ref), (plane_hbm, plane_ref),
             (offset_hbm, offset_ref), (vis_hbm, vis_ref), (table_hbm, table)]
        )
    ]
    for load in loads:
        load.start()
    for k in range(1, chans):
        other = lax.rem(chan + k, chans)
        pl.semaphore_signal(barrier, inc=1, device_id={"chan": other}, device_id_type=MESH)
        for z in (next_tile, prev_tile):
            pl.semaphore_signal(barrier, inc=1, device_id={"chan": other, "tile": z}, device_id_type=MESH)

    loads[0].wait()
    owner = tile_ref[...]
    marks = jnp.concatenate([jnp.where(owner == t, 1.0, 0.0) for t in range(tiles)], axis=0)
    size = tiles * blocks
    marks16 = marks.astype(jnp.bfloat16)
    before = ones_where(iota((LANES, LANES), 0) < iota((LANES, LANES), 1))
    inside = jnp.dot(marks16, before, preferred_element_type=jnp.float32)
    totals = jnp.dot(marks16, jnp.ones((LANES, LANES), jnp.bfloat16), preferred_element_type=jnp.float32)
    here, there = iota((size, size), 0), iota((size, size), 1)
    earlier = ones_where((here // blocks == there // blocks) & (there < here))
    ahead = jnp.dot(earlier, totals.astype(jnp.bfloat16), preferred_element_type=jnp.float32)
    ranks[...] = jnp.where(marks > 0.5, inside + ahead, -1.0)

    for load in loads[1:5]:
        load.wait()
    cell = cell_ref[...]
    vis = vis_ref[...]
    high = vis.astype(jnp.bfloat16).astype(jnp.float32)
    rows[0:2, :] = high
    rows[2:4, :] = vis - high
    for at, field in enumerate([plane_ref[...], offset_ref[...], cell // 256, cell & 255]):
        field = field.astype(jnp.float32)
        for b in range(blocks):
            rows[4 + at : 5 + at, b * LANES : (b + 1) * LANES] = field[b : b + 1, :]
    rows16 = rows[...].astype(jnp.bfloat16)

    slot = iota((CAPACITY, LANES), 0).astype(jnp.float32)
    for t in range(tiles):
        pick = jnp.concatenate(
            [ones_where(slot == ranks[t * blocks + b : t * blocks + b + 1, :]) for b in range(blocks)], axis=1)
        send_rows[t] = lax.dot_general(rows16, pick, NT, preferred_element_type=jnp.float32).astype(jnp.bfloat16)

    loads[5].wait()
    highs = table.shape[0] // LOW
    for h in range(highs):
        lookup[h * LANES : (h + 1) * LANES, :] = table[h * LOW : (h + 1) * LOW, :].T

    shifted = iota((LOW, LANES), 0).astype(jnp.float32) - LOW // 2
    ramp[...] = shifted.astype(jnp.bfloat16)
    coarse_ramp = iota((coarse, LANES), 0).astype(jnp.float32) - coarse // 2
    steps[...] = coarse_ramp.astype(jnp.bfloat16)

    def hot(reference, value, count):
        value = value.astype(jnp.float32).astype(jnp.bfloat16)
        return jnp.concatenate(
            [jnp.where(reference == value[:, n * LANES : (n + 1) * LANES], one, nil) for n in range(count)], axis=1)

    def spread_rows(blocks_in, chunk):
        count = len(blocks_in)
        got = jnp.concatenate([block.astype(jnp.float32) for block in blocks_in], axis=1)
        real, imag = got[0:1] + got[2:3], got[1:2] + got[3:4]
        whole = got.astype(jnp.int32)
        plane, offset = whole[4:5], whole[5:6]
        cell = whole[6:7] * 256 + whole[7:8]
        u, v = cell & (width - 1), cell // width
        pick = hot(ramp[...], (plane & 7) * 64 + offset - LOW // 2, count)
        found = jnp.dot(lookup[...], pick, preferred_element_type=jnp.float32)
        kern = found[0:LANES]
        for h in range(1, highs):
            kern = jnp.where(plane // 8 == h, found[h * LANES : (h + 1) * LANES], kern)
        kern_real, kern_imag = kern[:AREA], kern[AREA:]
        parts = [real * kern_real - imag * kern_imag, real * kern_imag + imag * kern_real]

        onehot[:, :chunk] = hot(steps[...], u // SUPPORT - coarse // 2, count)
        onehot[:, chunk : 2 * chunk] = hot(steps[...], u // SUPPORT + 1 - coarse // 2, count)
        fine = u & (SUPPORT - 1)
        row = iota((SUPPORT, chunk), 0)
        turn = (row - v) & (SUPPORT - 1)
        taps = []
        for i in range(SUPPORT):
            pair = [turned(part[8 * i : 8 * i + 8], v, turn) for part in parts]
            taps.append(jnp.concatenate(pair, axis=0).astype(jnp.bfloat16))
        zero = jnp.zeros((2 * SUPPORT, chunk), jnp.bfloat16)
        for bit in range(3):
            by = 1 << bit
            flag = jnp.where((jnp.broadcast_to(fine, (2 * SUPPORT, chunk)) & by) != 0, 1.0, 0.0)
            on = flag.astype(jnp.bfloat16) > nil
            later = [zero] * by + taps
            kept = taps + [zero] * by
            taps = [jnp.where(on, x, y) for x, y in zip(later, kept)]
        taps = taps + [zero]
        keep = []
        for k in range(3):
            inside = jnp.where((row + 8 * k >= v) & (row + 8 * k < v + SUPPORT), 1.0, 0.0)
            keep.append(jnp.concatenate([inside, inside], axis=0).astype(jnp.bfloat16))
        for f in range(2 * SUPPORT):
            lanes, place = pl.ds(f // SUPPORT * chunk, chunk), f % SUPPORT
            for k in range(3):
                at = place * 2 * TILE_V + k * 2 * SUPPORT if k < 2 else MAIN + place * 2 * SUPPORT
                spread[at : at + 2 * SUPPORT, lanes] = taps[f] * keep[k]

    spread_rows([send_rows[tile]], CAPACITY)
    sums[...] = lax.dot_general(
        onehot[:, : 2 * CAPACITY], spread[:, : 2 * CAPACITY], NT, preferred_element_type=jnp.float32)

    pl.semaphore_wait(barrier, tiles - 1 + 3 * (chans - 1))
    order = near_first(tiles)
    row_copies = {}
    for j in range(1, tiles):
        to = lax.rem(tile + order[j], tiles)
        row_copies[j] = pltpu.make_async_remote_copy(
            src_ref=send_rows.at[to], dst_ref=got_rows.at[j], send_sem=row_send.at[j], recv_sem=row_recv.at[j],
            device_id={"tile": to}, device_id_type=MESH)
        row_copies[j].start()

    main_copies, main_slots, edge_copies = [], [], []
    for first, end in groups_of(tiles)[1:]:
        chunk = (end - first) * CAPACITY
        for j in range(first, end):
            row_copies[j].wait_recv()
        spread_rows([got_rows[j] for j in range(first, end)], chunk)
        taps_on = spread[:, : 2 * chunk]
        if end < tiles:
            add = lax.dot_general(onehot[:, : 2 * chunk], taps_on, NT, preferred_element_type=jnp.float32)
            sums[...] = sums[...] + add
            continue
        for dy in reversed(near_first(chips_y)):
            to_y = lax.rem(at_y + dy, chips_y)
            window = pl.ds(pl.multiple_of(to_y * BLOCK, BLOCK), BLOCK)
            piece = sums[window, :] + lax.dot_general(
                onehot[window, : 2 * chunk], taps_on, NT, preferred_element_type=jnp.float32)
            piece = piece.astype(jnp.bfloat16)
            for k in range(NEAR):
                send_main[to_y * NEAR + k] = piece[k * COLS : (k + 1) * COLS, :MAIN]
                send_edge[to_y * NEAR + k] = piece[k * COLS : (k + 1) * COLS, MAIN:]
            edges = []
            for dx in reversed(near_first(CHIPS_X)):
                for dc in range(CORES):
                    k = dy * NEAR + dx * CORES + dc
                    to = to_y * NEAR + lax.rem(at_x + dx, CHIPS_X) * CORES + lax.rem(at_core + dc, CORES)
                    edges.append(pltpu.make_async_remote_copy(
                        src_ref=send_edge.at[to], dst_ref=got_edge.at[k], send_sem=edge_send.at[k],
                        recv_sem=edge_recv.at[k], device_id={"chan": to, "tile": next_tile}, device_id_type=MESH))
                    if k > 0:
                        main_copies.append(pltpu.make_async_remote_copy(
                            src_ref=send_main.at[to], dst_ref=got_main.at[k], send_sem=main_send.at[k],
                            recv_sem=main_recv.at[k], device_id={"chan": to}, device_id_type=MESH))
                        main_copies[-1].start()
                        main_slots.append(k)
            edge_copies += edges

    @pl.when(tile < tiles - 1)
    def _():
        for copy in edge_copies:
            copy.start()

    got_main[0] = send_main[chan]
    main = got_main[0].astype(jnp.float32)
    for copy, k in zip(main_copies, main_slots):
        copy.wait_recv()
        main = main + got_main[k].astype(jnp.float32)

    @pl.when(tile > 0)
    def _():
        for copy in edge_copies:
            copy.wait_recv()

    past = got_edge[0].astype(jnp.float32)
    for k in range(1, chans):
        past = past + got_edge[k].astype(jnp.float32)
    past = jnp.where(tile > 0, past, 0.0)

    main, past = main.T, past.T
    strips = []
    for f in range(SUPPORT):
        own = main[f * 2 * TILE_V : (f + 1) * 2 * TILE_V]
        edge = past[f * 2 * SUPPORT : (f + 1) * 2 * SUPPORT]
        low = own[: 2 * SUPPORT] + edge
        high = own[2 * SUPPORT :]
        strips.append(jnp.concatenate([low[:8], high[:8], low[8:], high[8:]], axis=0))
    mixed = jnp.concatenate(strips, axis=1)
    source, target = iota((LANES, LANES), 0), iota((LANES, LANES), 1)
    place = ones_where(target == (source & (COLS - 1)) * SUPPORT + source // COLS)
    grid = jnp.zeros((2 * TILE_V, LANES), jnp.float32)
    for _ in range(3):
        term = mixed.astype(jnp.bfloat16)
        grid = grid + jnp.dot(term, place, preferred_element_type=jnp.float32)
        mixed = mixed - term.astype(jnp.float32)
    for c in range(2):
        out_ref[c] = grid[c * TILE_V : (c + 1) * TILE_V]
    for copy in list(row_copies.values()) + main_copies:
        copy.wait_send()

    @pl.when(tile < tiles - 1)
    def _():
        for copy in edge_copies:
            copy.wait_send()


def body(visibility, kernel_table, cell_index, tile_index, plane_index, offset_index):
    chans, tiles = lax.axis_size("chan"), lax.axis_size("tile")
    count = cell_index.shape[0]
    blocks = count // LANES
    shape = (blocks, LANES)
    coarse = chans * COLS
    chunk = WIDEST * CAPACITY
    return pl.pallas_call(
        functools.partial(kernel, chans, tiles),
        out_shape=jax.ShapeDtypeStruct((2, TILE_V, LANES), jnp.float32),
        in_specs=[pl.BlockSpec(memory_space=pltpu.HBM)] * 6,
        out_specs=pl.BlockSpec(memory_space=pltpu.VMEM),
        scratch_shapes=[
            pltpu.VMEM((2, count), jnp.float32),
            pltpu.VMEM(shape, jnp.int32),
            pltpu.VMEM(shape, jnp.int32),
            pltpu.VMEM(shape, jnp.int32),
            pltpu.VMEM(shape, jnp.int32),
            pltpu.VMEM(kernel_table.shape, kernel_table.dtype),
            pltpu.VMEM((FIELDS, count), jnp.float32),
            pltpu.VMEM((tiles * blocks, LANES), jnp.float32),
            pltpu.VMEM((kernel_table.shape[0] // LOW * LANES, LOW), jnp.bfloat16),
            pltpu.VMEM((tiles, FIELDS, CAPACITY), jnp.bfloat16),
            pltpu.VMEM((tiles, FIELDS, CAPACITY), jnp.bfloat16),
            pltpu.VMEM((HALF, 2 * chunk), jnp.bfloat16),
            pltpu.VMEM((coarse, 2 * chunk), jnp.bfloat16),
            pltpu.VMEM((LOW, LANES), jnp.bfloat16),
            pltpu.VMEM((coarse, LANES), jnp.bfloat16),
            pltpu.VMEM((coarse, HALF), jnp.float32),
            pltpu.VMEM((chans, COLS, MAIN), jnp.bfloat16),
            pltpu.VMEM((chans, COLS, MAIN), jnp.bfloat16),
            pltpu.VMEM((chans, COLS, EDGE), jnp.bfloat16),
            pltpu.VMEM((chans, COLS, EDGE), jnp.bfloat16),
            pltpu.SemaphoreType.DMA((6,)),
            pltpu.SemaphoreType.DMA((tiles,)),
            pltpu.SemaphoreType.DMA((tiles,)),
            pltpu.SemaphoreType.DMA((chans,)),
            pltpu.SemaphoreType.DMA((chans,)),
            pltpu.SemaphoreType.DMA((chans,)),
            pltpu.SemaphoreType.DMA((chans,)),
        ],
        compiler_params=pltpu.CompilerParams(
            collective_id=0, has_side_effects=True, vmem_limit_bytes=60 * 1024 * 1024),
    )(visibility, cell_index.reshape(shape), tile_index.reshape(shape), plane_index.reshape(shape),
      offset_index.reshape(shape), kernel_table)


def solution(mesh):
    placed = (
        P(None, ("chan", "tile")),
        P(),
        P(("chan", "tile")),
        P(("chan", "tile"), None),
        P(("chan", "tile")),
        P(("chan", "tile")),
    )
    return jax.shard_map(
        body, mesh=mesh, in_specs=placed, out_specs=P(None, "tile", "chan"), check_vma=False
    )
```
